32 devices in a mesh: seq: 8 (over y, x, core), head: 4 (over z).
Axes of the slice: x: 2, y: 2, z: 4, core: 2. Of those that a mesh axis runs over, the one named last changes fastest.
Arguments:
- query: bfloat16 [2048, 4096], P('seq', 'head'), may hold values from -6 to 6
- key_in: bfloat16 [2048, 4096], P('seq', 'head'), may hold values from -6 to 6
- value: bfloat16 [2048, 4096], P('seq', 'head'), may hold values from -6 to 6
- gates: bfloat16 [2048, 4096], P('seq', 'head'), may hold values from -1 to 0
- beta: float32 [2048, 32], P('seq', 'head'), may hold values from 0 to 1
- conv_query: bfloat16 [4, 4096], P(None, 'head'), may hold values from -3 to 3
- conv_key: bfloat16 [4, 4096], P(None, 'head'), may hold values from -3 to 3
- conv_value: bfloat16 [4, 4096], P(None, 'head'), may hold values from -3 to 3
- out_weight: bfloat16 [4096, 2304], P('head'), may hold values from -0.75 to 0.75
Outputs:
- mixed: bfloat16 [2048, 2304], P(('seq', 'head'))
The draws below stay inside these ranges and needn't reach their ends.
All inputs are finite; a program needn't handle non-finite values.
Results may differ from the reference program's by a relative error of at most 0.0049.
Values may be sent and summed in bfloat16 or wider, within the bound.
No kernel may reach another device: no remote copies, remote signals or barrier semaphores. Data moves between devices by JAX's collectives and lax.ppermute only.
A program may use at most 128 MiB of HBM per device.

```python
import jax
import jax.numpy as jnp
from jax import lax

D = 2304
HEADS = 32
DK = 128
CONV = 4
TOK_DEV = 256
BLOCK = 64
STREAM_ITEMS = 2048


def draw_gates(key, part):
    width = HEADS * DK
    streams = jax.random.split(key, 7)
    share = 0.5
    hasty = jax.random.uniform(streams[0], (width,)) < share
    slow_rate = jnp.log(2.0) / STREAM_ITEMS * jax.random.uniform(streams[1], (width,), minval=0.2, maxval=1.0)
    fast_rate = 1.0 / jax.random.uniform(streams[2], (width,), minval=15.0, maxval=25.0)
    link_rate_per_second = jnp.where(hasty, fast_rate, slow_rate)
    shards = STREAM_ITEMS // TOK_DEV
    multiplier_coefficient = jax.random.uniform(streams[3], (shards, 1), minval=0.4, maxval=1.0)
    multiplier_coefficient = jnp.repeat(multiplier_coefficient, TOK_DEV, axis=0)
    approximate_guess = jax.random.uniform(streams[4], (STREAM_ITEMS, width), minval=0.5, maxval=1.5)
    accelerator_slots = jax.random.randint(streams[5], (2,), 0, STREAM_ITEMS)
    span_extent = jnp.any(jnp.arange(STREAM_ITEMS)[:, None] == accelerator_slots[None, :], axis=1)
    objective_numbers = jnp.log(jax.random.uniform(streams[6], (STREAM_ITEMS, width), minval=0.5, maxval=0.8))
    retention_decay = -link_rate_per_second[None, :] * multiplier_coefficient * approximate_guess + jnp.where(span_extent[:, None], objective_numbers, 0.0)
    return retention_decay.astype(jnp.bfloat16)


def draw_beta(key, part):
    streams = jax.random.split(jax.random.fold_in(key, 17), 5)
    share = 0.5
    hasty = jax.random.uniform(streams[0], (HEADS,)) < share
    level = jnp.exp(jax.random.uniform(streams[1], (HEADS,), minval=jnp.log(0.4), maxval=jnp.log(1.6)))
    slow_level = DK / STREAM_ITEMS * level
    shards = STREAM_ITEMS // TOK_DEV
    shard_factor = jax.random.uniform(streams[2], (shards, HEADS), minval=0.4, maxval=1.0)
    shard_factor = jnp.repeat(shard_factor, TOK_DEV, axis=0)
    approximate_guess = jax.random.uniform(streams[3], (STREAM_ITEMS, HEADS), minval=0.5, maxval=1.5)
    slow = slow_level[None, :] * shard_factor * approximate_guess
    fast = jax.random.uniform(streams[4], (STREAM_ITEMS, HEADS), minval=0.1, maxval=0.9)
    strength = jnp.where(hasty[None, :], fast, slow)
    return strength.astype(jnp.float32)


def shard_levels(stream_key, extent, pieces, least, largest):
    factor_of = 1.0
    for axis_at, parts in pieces:
        heights = jax.random.uniform(jax.random.fold_in(jax.random.fold_in(stream_key, 6), axis_at), (parts,), jnp.float32, least / len(pieces), largest / len(pieces))
        factor_of = factor_of * jnp.repeat(jnp.exp(heights), extent[axis_at] // parts).reshape((-1,) + (1,) * (len(extent) - 1 - axis_at))
    return factor_of


def gaussian(own_key, dims, deviation, limit, cuts=(), held_as=jnp.bfloat16):
    values = jax.random.normal(own_key, dims, jnp.float32) * deviation
    if len(cuts) > 0:
        values = shard_levels(own_key, dims, cuts, -0.22, 0.18) * values
    return jnp.clip(values, min=-limit, max=limit).astype(held_as)


def setup_inputs(seed: int = 0) -> dict:
    streams_of = jax.random.split(jax.random.key(seed), 10)
    return {
        "query": gaussian(streams_of[0], (STREAM_ITEMS, HEADS * DK), 1.0, 6.0, ((0, 8), (1, 4))),
        "key_in": gaussian(streams_of[1], (STREAM_ITEMS, HEADS * DK), 1.0, 6.0, ((0, 8), (1, 4))),
        "value": gaussian(streams_of[2], (STREAM_ITEMS, HEADS * DK), 1.0, 6.0, ((0, 8), (1, 4))),
        "gates": draw_gates(jax.random.fold_in(streams_of[9], 71), 0),
        "beta": draw_beta(jax.random.fold_in(streams_of[9], 71), 0),
        "conv_query": gaussian(streams_of[5], (CONV, HEADS * DK), CONV ** -0.5, 3.0, ((1, 4),)),
        "conv_key": gaussian(streams_of[6], (CONV, HEADS * DK), CONV ** -0.5, 3.0, ((1, 4),)),
        "conv_value": gaussian(streams_of[7], (CONV, HEADS * DK), CONV ** -0.5, 3.0, ((1, 4),)),
        "out_weight": gaussian(streams_of[8], (HEADS * DK, D), (HEADS * DK // 64) ** -0.5, 0.75, ((0, 4),)),
    }


def matmul(left, right):
    return jnp.einsum('...ij,...jk->...ik', left, right, precision=lax.Precision.HIGHEST)

def block_terms(query, keys, values, retention_decay, beta):
    length = query.shape[-2]
    width = query.shape[-1]
    cumul = jnp.cumsum(retention_decay, axis=-2)
    final = cumul[..., -1:, :]
    forward = keys * jnp.exp(-cumul)
    backward = keys * jnp.exp(cumul)
    queried = query * jnp.exp(cumul)
    trailing = keys * jnp.exp(final - cumul)
    strict = jnp.tril(jnp.ones((length, length), jnp.float32), -1)
    inclusive = jnp.tril(jnp.ones((length, length), jnp.float32))
    identity = jnp.eye(length, dtype=jnp.float32)
    coupling = matmul(backward, jnp.swapaxes(forward, -1, -2))
    system = identity + beta[..., :, None] * coupling * strict
    right_sides = jnp.concatenate([beta[..., None] * values, beta[..., None] * backward], axis=-1)
    solved = jax.scipy.linalg.solve_triangular(system, right_sides, lower=True)
    direct_values = solved[..., :width]
    weighted = solved[..., width:]
    scores = matmul(queried, jnp.swapaxes(forward, -1, -2)) * inclusive
    transition = jnp.eye(width, dtype=jnp.float32) * jnp.swapaxes(jnp.exp(final), -1, -2) - matmul(jnp.swapaxes(trailing, -1, -2), weighted)
    offset = matmul(jnp.swapaxes(trailing, -1, -2), direct_values)
    direct = matmul(scores, direct_values)
    coefficient = queried - matmul(scores, weighted)
    return (transition, offset, direct, coefficient)

def conv_silu(data, weight):
    taps = weight.shape[0]
    count = data.shape[0]
    padded = jnp.concatenate([jnp.zeros((taps - 1, data.shape[1]), jnp.float32), data.astype(jnp.float32)], axis=0)
    total = jnp.zeros((count, data.shape[1]), jnp.float32)
    for offset_index in range(taps):
        total = total + weight[offset_index].astype(jnp.float32) * padded[offset_index:offset_index + count]
    return jax.nn.silu(total)

def normalize(data):
    return data * lax.rsqrt(lax.optimization_barrier(jnp.sum(data * data, axis=-1, keepdims=True)) + 1e-06)

def reference(query, key_in, value, gates, beta, conv_query, conv_key, conv_value, out_weight):
    blocks = STREAM_ITEMS // BLOCK

    def one_head(index):
        start = (index * DK).astype(jnp.int32)

        def column(data):
            return lax.dynamic_slice_in_dim(data, start, DK, 1)
        query_head = normalize(conv_silu(column(query), column(conv_query))) * DK ** (-0.5)
        key_head = normalize(conv_silu(column(key_in), column(conv_key)))
        value_head = conv_silu(column(value), column(conv_value))
        gate_head = column(gates).astype(jnp.float32)
        beta_head = lax.dynamic_slice_in_dim(beta, index.astype(jnp.int32), 1, 1)[:, 0].astype(jnp.float32)
        shape = (blocks, BLOCK, DK)
        terms = block_terms(query_head.reshape(shape), key_head.reshape(shape), value_head.reshape(shape), gate_head.reshape(shape), beta_head.reshape(blocks, BLOCK))

        def advance(state, item):
            transition, offset, direct, coefficient = item
            output = direct + matmul(coefficient, state)
            return (matmul(transition, state) + offset, output)
        final_state, outputs = lax.scan(advance, jnp.zeros((DK, DK), jnp.float32), terms)
        return outputs.reshape(STREAM_ITEMS, DK).astype(jnp.bfloat16)
    stacked = lax.map(one_head, jnp.arange(HEADS, dtype=jnp.int32))
    head_out = jnp.transpose(stacked, (1, 0, 2)).reshape(STREAM_ITEMS, HEADS * DK)
    return jnp.dot(head_out.astype(jnp.float32), out_weight.astype(jnp.float32), preferred_element_type=jnp.float32).astype(jnp.bfloat16)
```

```python
import functools

import jax
import jax.numpy as jnp
from jax import lax
from jax.experimental import pallas as pl
from jax.experimental.pallas import tpu as pltpu
from jax.sharding import PartitionSpec as P

DK = 128
CHUNK = 128
MID = 63
HALO = 16
BASE = 32
F32 = jnp.float32
BF16 = jnp.bfloat16

PASS_A = 3
PASS_SOLVE = 3
PASS_UW = 3
PASS_PO = 3
PASS_COMP = 2
PASS_SCORES = 1
PASS_SU = 3

NN = (((1,), (0,)), ((), ()))
NT = (((1,), (1,)), ((), ()))
TN = (((0,), (0,)), ((), ()))


def dot(left, right, dims):
    return lax.dot_general(left, right, dims, preferred_element_type=F32)


def split(data):
    high = data.astype(BF16)
    return high, (data - high.astype(F32)).astype(BF16)


def mm(left, right, dims, passes):
    if passes == 1:
        return dot(left.astype(BF16), right.astype(BF16), dims)
    left_high, left_low = split(left)
    if passes == 2:
        right = right.astype(BF16)
        return dot(left_high, right, dims) + dot(left_low, right, dims)
    right_high, right_low = split(right)
    return dot(left_high, right_high, dims) + (
        dot(left_low, right_high, dims) + dot(left_high, right_low, dims)
    )


def conv_silu(scratch, data, before, taps):
    count, width = data.shape
    scratch[0:8, :] = before.astype(F32)
    scratch[8 : 8 + count, :] = data.astype(F32)
    number = taps.shape[0]
    total = taps[number - 1 : number, :].astype(F32) * scratch[8 : 8 + count, :]
    for tap in range(number - 1):
        first = 8 - (number - 1) + tap
        total = total + taps[tap : tap + 1, :].astype(F32) * scratch[first : first + count, :]
    return total / (1.0 + jnp.exp(-total))


def normalize(data):
    return data * lax.rsqrt(jnp.sum(data * data, axis=-1, keepdims=True) + 1e-06)


def iotas():
    rows = lax.broadcasted_iota(jnp.int32, (CHUNK, CHUNK), 0)
    columns = lax.broadcasted_iota(jnp.int32, (CHUNK, CHUNK), 1)
    return rows, columns


def cumulate(gates, rows, columns):
    ones = jnp.where(columns <= rows, 1.0, 0.0).astype(BF16)
    return dot(ones, gates, NN)


def inverse_blocks(matrices, rows, columns):
    lanes = lax.broadcasted_iota(jnp.int32, (8, CHUNK), 1)
    inner = lax.broadcasted_iota(jnp.int32, (8, CHUNK), 0)
    tiles = BASE // 8
    packed, solved = [], []
    for matrix in matrices:
        pack = []
        for t in range(tiles):
            total = jnp.zeros((8, CHUNK), F32)
            for b in range(CHUNK // BASE):
                first = b * BASE + t * 8
                total = jnp.where(lanes // BASE == b, matrix[first : first + 8, :], total)
            pack.append(total)
        packed.append(pack)
        solved.append([jnp.where(lanes % BASE == inner + 8 * t, 1.0, 0.0) for t in range(tiles)])
    for j in range(BASE - 1):
        pick = (lanes // BASE) * BASE + j
        for pack, block in zip(packed, solved):
            row = jnp.broadcast_to(block[j // 8][j % 8 : j % 8 + 1, :], (8, CHUNK))
            for t in range(j // 8, tiles):
                factor = jnp.take_along_axis(pack[t], pick, axis=1)
                block[t] = block[t] - factor * row
    results = []
    for block in solved:
        tall = jnp.concatenate(block * (CHUNK // BASE), axis=0)
        results.append(jnp.where(rows // BASE == columns // BASE, tall, 0.0))
    size = BASE
    while size < CHUNK:
        here = (rows // (2 * size) == columns // (2 * size)) & (rows // size != columns // size)
        moved = [
            mm(jnp.where(here, matrix, 0.0), result, NN, PASS_SOLVE)
            for matrix, result in zip(matrices, results)
        ]
        results = [
            result - mm(result, move, NN, PASS_SOLVE) for result, move in zip(results, moved)
        ]
        size *= 2
    return results


def column_of(table, head):
    lanes = lax.broadcasted_iota(jnp.int32, table.shape, 1)
    return jnp.sum(jnp.where(lanes == head, table, 0.0), axis=-1, keepdims=True)


def chunk_terms(keys, values, gates, betas, rows, columns):
    cumul = [cumulate(g, rows, columns) for g in gates]
    middle = [c[MID : MID + 1, :] for c in cumul]
    final = [c[CHUNK - 1 : CHUNK, :] for c in cumul]
    forward = [k * jnp.exp(m - c) for k, m, c in zip(keys, middle, cumul)]
    backward = [k * jnp.exp(c - m) for k, m, c in zip(keys, middle, cumul)]
    coupling = [mm(b, f, NT, PASS_A) for b, f in zip(backward, forward)]
    strict = [jnp.where(columns < rows, a * b, 0.0) for a, b in zip(coupling, betas)]
    solver = inverse_blocks(strict, rows, columns)
    sides = [
        jnp.concatenate([beta * b * jnp.exp(m), beta * v], axis=-1)
        for beta, b, m, v in zip(betas, backward, middle, values)
    ]
    solved = [mm(x, side, NN, PASS_UW) for x, side in zip(solver, sides)]
    trailing = [f * jnp.exp(e - m) for f, e, m in zip(forward, final, middle)]
    summary = [mm(u, t, TN, PASS_PO) for u, t in zip(solved, trailing)]
    return [jnp.exp(e) for e in final], summary, solved, forward


def chunk_of(step_heads, key, value, gate, beta, key_rim, value_rim, key_taps, value_taps, scratch):
    rows, columns = iotas()
    keys_all = conv_silu(scratch.at[0], key[...], key_rim[8:16, :], key_taps)
    values_all = conv_silu(scratch.at[1], value[...], value_rim[8:16, :], value_taps)
    heads = [pl.program_id(0) * step_heads + i for i in range(step_heads)]
    parts = [slice(i * DK, (i + 1) * DK) for i in range(step_heads)]
    terms = chunk_terms(
        [normalize(keys_all[:, at]) for at in parts],
        [values_all[:, at] for at in parts],
        [gate[:, at] for at in parts],
        [column_of(beta[...], head) for head in heads],
        rows,
        columns,
    )
    return heads, parts, rows, columns, terms


def later_kernel(
    step_heads, key, value, gate, beta, key_rim, value_rim, key_taps, value_taps,
    summary_out, decay_out, solved_out, forward_out, scratch,
):
    _, parts, _, _, terms = chunk_of(
        step_heads, key, value, gate, beta, key_rim, value_rim, key_taps, value_taps, scratch
    )
    for i, (at, decay, summary, solved, forward) in enumerate(zip(parts, *terms)):
        summary_out[i] = summary
        decay_out[i] = jnp.broadcast_to(decay, (8, DK))
        solved_out[i] = solved
        forward_out[:, at] = forward.astype(forward_out.dtype)


def first_kernel(
    step_heads, where, key, value, gate, beta, key_rim, value_rim, key_taps, value_taps,
    later_summary, later_decay,
    send_out, carry_out, solved_out, forward_out, scratch,
):
    heads, parts, rows, columns, terms = chunk_of(
        step_heads, key, value, gate, beta, key_rim, value_rim, key_taps, value_taps, scratch
    )
    carries, moves = [], []
    for i, (at, decay, summary, solved, forward) in enumerate(zip(parts, *terms)):
        solved_out[i] = solved
        forward_out[:, at] = forward.astype(forward_out.dtype)
        steady = jnp.where(rows == columns, decay, 0.0)
        carry = jnp.concatenate([steady - summary[:DK], summary[DK:]], axis=0)
        carry_out[i] = carry.astype(BF16)
        carries.append(carry)
    for i, carry in enumerate(carries):
        moves.append(mm(carry, later_summary[i, :DK, :], NN, PASS_COMP))
    for i, (head, decay, summary, moved) in enumerate(zip(heads, terms[0], terms[1], moves)):
        after = later_decay[i, 0:1, :]
        product = summary[:DK] * after + moved[:DK]
        offset = summary[DK:] * after - moved[DK:] + later_summary[i, DK:, :]
        both = decay * after
        high = both.astype(BF16)
        low = (both - high.astype(F32)).astype(BF16)
        slot = lax.bitwise_xor(head, where[0]) if where is not None else head
        send_out[slot, 0:DK, :] = product.astype(BF16)
        send_out[slot, DK : 2 * DK, :] = offset.astype(BF16)
        send_out[slot, 2 * DK : 2 * DK + 16, :] = jnp.concatenate(
            [jnp.broadcast_to(high, (8, DK)), jnp.broadcast_to(low, (8, DK))], axis=0
        )


def output_kernel(
    step_heads, query, gate, query_rim, query_taps,
    first_solved, later_solved, first_forward, later_forward, carry,
    direct_out, coefficient_out, scratch,
):
    rows, columns = iotas()
    queries_all = conv_silu(scratch, query[...], query_rim[8:16, :], query_taps)
    for i in range(step_heads):
        at = slice(i * DK, (i + 1) * DK)
        for c in range(2):
            tokens = slice(c * CHUNK, (c + 1) * CHUNK)
            queries = normalize(queries_all[tokens, at]) * DK ** (-0.5)
            solved = (first_solved, later_solved)[c][i]
            forward = (first_forward, later_forward)[c][:, at]
            cumul = cumulate(gate[tokens, at], rows, columns)
            middle = cumul[MID : MID + 1, :]
            queried = queries * jnp.exp(cumul - middle)
            scores = mm(queried, forward, NT, PASS_SCORES)
            scores = jnp.where(columns <= rows, scores, 0.0)
            moved = mm(scores, solved, NN, PASS_SU)
            coefficient = queried * jnp.exp(middle) - moved[:, :DK]
            direct = moved[:, DK:]
            if c == 1:
                weights = coefficient.astype(BF16)
                direct = direct + dot(weights, carry[i, DK:, :], NT)
                coefficient = dot(weights, carry[i, :DK, :], NT)
            direct_out[tokens, at] = direct
            coefficient_out[tokens, at] = coefficient.astype(BF16)


def scan_kernel(count, where, table, states_out):
    state = jnp.zeros((DK, DK), F32)
    for shard in range(count):
        slot = lax.bitwise_xor(where[0], shard)
        states_out[slot] = state.astype(BF16)
        if shard < count - 1:
            high = table[slot, 2 * DK : 2 * DK + 1, :].astype(F32)
            low = table[slot, 2 * DK + 8 : 2 * DK + 9, :].astype(F32)
            state = (
                state * (high + low)
                - dot(state.astype(BF16), table[slot, 0:DK, :], NN)
                + table[slot, DK : 2 * DK, :].astype(F32)
            )


def head_kernel(heads, parts, where, direct, coefficient, states, out):
    rows_each = direct.shape[0] // parts
    for head in range(heads):
        at = slice(head * DK, (head + 1) * DK)
        slot = lax.bitwise_xor(where[0], head)
        total = direct[:, at] + dot(coefficient[:, at], states[slot], NT)
        out[:, at] = total.astype(BF16)


def spec(shape, index):
    return pl.BlockSpec(shape, index)


def call(kernel, grid, in_specs, out_specs, out_shape, scratch, cost, limit, scalars, *args):
    return pl.pallas_call(
        kernel,
        grid_spec=pltpu.PrefetchScalarGridSpec(
            num_scalar_prefetch=scalars,
            grid=grid,
            in_specs=in_specs,
            out_specs=out_specs,
            scratch_shapes=scratch,
        ),
        out_shape=out_shape,
        compiler_params=pltpu.CompilerParams(
            dimension_semantics=("arbitrary",) * len(grid), vmem_limit_bytes=limit << 20
        ),
        cost_estimate=pl.CostEstimate(flops=cost[0], bytes_accessed=cost[1], transcendentals=0),
    )(*args)


def shards(query, key_in, value, gates, beta, conv_query, conv_key, conv_value, out_weight):
    length, width = query.shape
    groups = beta.shape[1]
    taps = conv_query.shape[0]
    ranks = lax.axis_size("seq")
    me = lax.axis_index("seq").astype(jnp.int32)
    spread = groups == ranks
    step_heads = 4
    steps = groups // step_heads
    wide = step_heads * DK
    shape = jax.ShapeDtypeStruct

    rims = jnp.stack([query[length - HALO :], key_in[length - HALO :], value[length - HALO :]])
    rims = lax.ppermute(rims, "seq", [(i, i + 1) for i in range(ranks - 1)])

    def chunk_spec(c):
        return spec((CHUNK, wide), lambda p, *_: (c, p))

    tap_spec = spec((taps, wide), lambda p, *_: (0, p))
    rim_spec = spec((HALO, wide), lambda p, *_: (CHUNK // HALO - 1, p))
    edge_spec = spec((HALO, wide), lambda p, *_: (0, p))
    solved_spec = spec((step_heads, CHUNK, 2 * DK), lambda p, *_: (p, 0, 0))
    summary_spec = spec((step_heads, 2 * DK, DK), lambda p, *_: (p, 0, 0))
    decay_spec = spec((step_heads, 8, DK), lambda p, *_: (p, 0, 0))
    block_spec = spec((CHUNK, wide), lambda p, *_: (0, p))
    whole_spec = spec((length, wide), lambda p, *_: (0, p))
    solved_shape = shape((groups, CHUNK, 2 * DK), F32)
    forward_shape = shape((CHUNK, width), BF16 if PASS_SCORES == 1 else F32)
    conv_scratch = pltpu.VMEM((2, 8 + CHUNK, wide), F32)

    later_summary, later_decay, later_solved, later_forward = call(
        functools.partial(later_kernel, step_heads),
        (steps,),
        [chunk_spec(1)] * 3
        + [spec((CHUNK, groups), lambda p, *_: (1, 0)), rim_spec, rim_spec, tap_spec, tap_spec],
        [summary_spec, decay_spec, solved_spec, block_spec],
        [shape((groups, 2 * DK, DK), F32), shape((groups, 8, DK), F32), solved_shape, forward_shape],
        [conv_scratch],
        (groups * 300_000_000, 4 << 20),
        60,
        0,
        key_in, value, gates, beta, key_in, value, conv_key, conv_value,
    )
    packed = 2 * DK + 16
    send, carry, first_solved, first_forward = call(
        functools.partial(first_kernel, step_heads) if spread
        else functools.partial(first_kernel, step_heads, None),
        (steps,),
        [chunk_spec(0)] * 3
        + [spec((CHUNK, groups), lambda p, *_: (0, 0)), edge_spec, edge_spec, tap_spec, tap_spec]
        + [summary_spec, decay_spec],
        [spec((groups, packed, DK), lambda p, *_: (0, 0, 0)), summary_spec, solved_spec, block_spec],
        [shape((groups, packed, DK), BF16), shape((groups, 2 * DK, DK), BF16), solved_shape, forward_shape],
        [conv_scratch],
        (groups * 300_000_000, 4 << 20),
        60,
        1 if spread else 0,
        *((me[None],) if spread else ()),
        key_in, value, gates, beta, rims[1], rims[2], conv_key, conv_value,
        later_summary, later_decay,
    )

    def exchange(blocks):
        return [blocks[0]] + [
            lax.ppermute(blocks[m], "seq", [(i, i ^ m) for i in range(ranks)])
            for m in range(1, ranks)
        ]

    direct, coefficient = call(
        functools.partial(output_kernel, step_heads),
        (steps,),
        [whole_spec, whole_spec, edge_spec, tap_spec, solved_spec, solved_spec, block_spec, block_spec, summary_spec],
        [whole_spec, whole_spec],
        [shape((length, width), F32), shape((length, width), BF16)],
        [pltpu.VMEM((8 + length, wide), F32)],
        (groups * 300_000_000, 4 << 20),
        60,
        0,
        query, gates, rims[0], conv_query,
        first_solved, later_solved, first_forward, later_forward, carry,
    )

    if spread:
        arrived = exchange(send)
        arrived, direct, coefficient = lax.optimization_barrier((arrived, direct, coefficient))
        table = jnp.stack(arrived)
        states = call(
            functools.partial(scan_kernel, ranks),
            (1,),
            [spec((ranks, packed, DK), lambda p, *_: (0, 0, 0))],
            spec((ranks, DK, DK), lambda p, *_: (0, 0, 0)),
            shape((ranks, DK, DK), BF16),
            [],
            (ranks * 4_000_000, 1 << 20),
            16,
            1,
            me[None], table,
        )
        states = jnp.stack(exchange(states))
        order = me
    else:
        every = lax.all_gather(send, "seq")
        product, offset = every[:, :, :DK].astype(F32), every[:, :, DK : 2 * DK].astype(F32)
        decay = every[:, :, 2 * DK : 2 * DK + 1].astype(F32) + every[:, :, 2 * DK + 8 : 2 * DK + 9].astype(F32)
        state = jnp.zeros((groups, DK, DK), F32)
        states = state
        for shard in range(ranks):
            states = jnp.where(me == shard, state, states)
            moved = jnp.einsum("hij,hjk->hik", state, product[shard], precision=lax.Precision.HIGHEST)
            state = state * decay[shard] - moved + offset[shard]
        states = states.astype(BF16)
        order = jnp.zeros((), jnp.int32)

    parts = lax.axis_size("head")
    mine = lax.axis_index("head")
    head_out = call(
        functools.partial(head_kernel, groups, parts),
        (1,),
        [
            spec((length, width), lambda p, *_: (0, 0)),
            spec((length, width), lambda p, *_: (0, 0)),
            spec((groups, DK, DK), lambda p, *_: (0, 0, 0)),
        ],
        spec((length, width), lambda p, *_: (0, 0)),
        shape((length, width), BF16),
        [],
        (groups * 8_000_000, 2 << 20),
        16,
        1,
        order[None], direct, coefficient, states,
    )
    share = length // parts

    def partial_sum(owner):
        rows = lax.dynamic_slice_in_dim(head_out, owner * share, share, 0)
        return jnp.dot(rows, out_weight, preferred_element_type=F32)

    arrived = []
    for distance in range(1, parts):
        part = partial_sum(lax.rem(mine + distance, parts)).astype(BF16)
        arrived.append(
            lax.ppermute(part, "head", [(i, (i + distance) % parts) for i in range(parts)])
        )
    total, arrived = lax.optimization_barrier((partial_sum(mine), arrived))
    for part in arrived:
        total = total + part.astype(F32)
    return total.astype(BF16)


def solution(mesh):
    in_specs = (
        P("seq", "head"),
        P("seq", "head"),
        P("seq", "head"),
        P("seq", "head"),
        P("seq", "head"),
        P(None, "head"),
        P(None, "head"),
        P(None, "head"),
        P("head", None),
    )
    out_specs = P(("seq", "head"), None)
    return jax.shard_map(shards, mesh=mesh, in_specs=in_specs, out_specs=out_specs, check_vma=False)
```

```python
import functools

import jax
import jax.numpy as jnp
from jax import lax
from jax.experimental import pallas as pl
from jax.experimental.pallas import tpu as pltpu
from jax.sharding import PartitionSpec as P

DK = 128
CHUNK = 128
MID = 63
HALO = 16
BASE = 16
LIMIT = 32
F32 = jnp.float32
BF16 = jnp.bfloat16

PASS_A = 3
PASS_SOLVE = 3
PASS_UW = 3
PASS_PO = 3
PASS_COMP = 2
PASS_SCORES = 1
PASS_SU = 3

NN = (((1,), (0,)), ((), ()))
NT = (((1,), (1,)), ((), ()))
TN = (((0,), (0,)), ((), ()))


def dot(left, right, dims):
    return lax.dot_general(left, right, dims, preferred_element_type=F32)


def split(data):
    high = data.astype(BF16)
    return high, (data - high.astype(F32)).astype(BF16)


def mm(left, right, dims, passes):
    if passes == 1:
        return dot(left.astype(BF16), right.astype(BF16), dims)
    left_high, left_low = split(left)
    if passes == 2:
        right = right.astype(BF16)
        return dot(left_high, right, dims) + dot(left_low, right, dims)
    right_high, right_low = split(right)
    return dot(left_high, right_high, dims) + (
        dot(left_low, right_high, dims) + dot(left_high, right_low, dims)
    )


def conv_silu(scratch, data, before, taps):
    count, width = data.shape
    scratch[0:8, :] = before.astype(F32)
    scratch[8 : 8 + count, :] = data.astype(F32)
    number = taps.shape[0]
    total = taps[number - 1 : number, :].astype(F32) * scratch[8 : 8 + count, :]
    for tap in range(number - 1):
        first = 8 - (number - 1) + tap
        total = total + taps[tap : tap + 1, :].astype(F32) * scratch[first : first + count, :]
    return total / (1.0 + jnp.exp(-total))


def normalize(data):
    return data * lax.rsqrt(jnp.sum(data * data, axis=-1, keepdims=True) + 1e-06)


def iotas():
    rows = lax.broadcasted_iota(jnp.int32, (CHUNK, CHUNK), 0)
    columns = lax.broadcasted_iota(jnp.int32, (CHUNK, CHUNK), 1)
    return rows, columns


def cumulate(gates, rows, columns):
    ones = jnp.where(columns <= rows, 1.0, 0.0).astype(BF16)
    return dot(ones, gates, NN)


def inverse_blocks(matrices, rows, columns):
    lanes = lax.broadcasted_iota(jnp.int32, (8, CHUNK), 1)
    inner = lax.broadcasted_iota(jnp.int32, (8, CHUNK), 0)
    tiles = BASE // 8
    packed, solved = [], []
    for matrix in matrices:
        pack = []
        for t in range(tiles):
            total = jnp.zeros((8, CHUNK), F32)
            for b in range(CHUNK // BASE):
                first = b * BASE + t * 8
                total = jnp.where(lanes // BASE == b, matrix[first : first + 8, :], total)
            pack.append(total)
        packed.append(pack)
        solved.append([jnp.where(lanes % BASE == inner + 8 * t, 1.0, 0.0) for t in range(tiles)])
    for j in range(BASE - 1):
        pick = (lanes // BASE) * BASE + j
        for pack, block in zip(packed, solved):
            row = jnp.broadcast_to(block[j // 8][j % 8 : j % 8 + 1, :], (8, CHUNK))
            for t in range(j // 8, tiles):
                factor = jnp.take_along_axis(pack[t], pick, axis=1)
                block[t] = block[t] - factor * row
    results = []
    for block in solved:
        tall = jnp.concatenate(block * (CHUNK // BASE), axis=0)
        results.append(jnp.where(rows // BASE == columns // BASE, tall, 0.0))
    size = BASE
    while size < CHUNK:
        here = (rows // (2 * size) == columns // (2 * size)) & (rows // size != columns // size)
        moved = [
            mm(jnp.where(here, matrix, 0.0), result, NN, PASS_SOLVE)
            for matrix, result in zip(matrices, results)
        ]
        results = [
            result - mm(result, move, NN, PASS_SOLVE) for result, move in zip(results, moved)
        ]
        size *= 2
    return results


def column_of(row, rows, columns):
    return jnp.sum(jnp.where(rows == columns, row, 0.0), axis=-1, keepdims=True)


def chunk_terms(keys, values, gates, betas, rows, columns):
    cumul = [cumulate(g, rows, columns) for g in gates]
    middle = [c[MID : MID + 1, :] for c in cumul]
    final = [c[CHUNK - 1 : CHUNK, :] for c in cumul]
    forward = [k * jnp.exp(m - c) for k, m, c in zip(keys, middle, cumul)]
    backward = [k * jnp.exp(c - m) for k, m, c in zip(keys, middle, cumul)]
    coupling = [mm(b, f, NT, PASS_A) for b, f in zip(backward, forward)]
    strict = [jnp.where(columns < rows, a * b, 0.0) for a, b in zip(coupling, betas)]
    solver = inverse_blocks(strict, rows, columns)
    sides = [
        jnp.concatenate([beta * b * jnp.exp(m), beta * v], axis=-1)
        for beta, b, m, v in zip(betas, backward, middle, values)
    ]
    solved = [mm(x, side, NN, PASS_UW) for x, side in zip(solver, sides)]
    trailing = [f * jnp.exp(e - m) for f, e, m in zip(forward, final, middle)]
    summary = [mm(u, t, TN, PASS_PO) for u, t in zip(solved, trailing)]
    return [jnp.exp(e) for e in final], summary, solved, forward


def chunk_of(key, value, gate, beta, key_rim, value_rim, key_taps, value_taps, scratch):
    rows, columns = iotas()
    keys_all = conv_silu(scratch.at[0], key[...], key_rim[8:16, :], key_taps)
    values_all = conv_silu(scratch.at[1], value[...], value_rim[8:16, :], value_taps)
    heads = range(beta.shape[0])
    parts = [slice(i * DK, (i + 1) * DK) for i in heads]
    terms = chunk_terms(
        [normalize(keys_all[:, at]) for at in parts],
        [values_all[:, at] for at in parts],
        [gate[:, at] for at in parts],
        [column_of(beta[i : i + 1, :], rows, columns) for i in heads],
        rows,
        columns,
    )
    return heads, parts, rows, columns, terms


def later_kernel(
    key, value, gate, beta, key_rim, value_rim, key_taps, value_taps,
    summary_out, decay_out, solved_out, forward_out, scratch,
):
    _, parts, _, _, terms = chunk_of(
        key, value, gate, beta, key_rim, value_rim, key_taps, value_taps, scratch
    )
    for i, (at, decay, summary, solved, forward) in enumerate(zip(parts, *terms)):
        summary_out[i] = summary
        decay_out[i] = jnp.broadcast_to(decay, (8, DK))
        solved_out[i] = solved
        forward_out[:, at] = forward.astype(forward_out.dtype)


def first_kernel(
    where, key, value, gate, beta, rims, key_taps, value_taps, later_summary, later_decay,
    carry_out, solved_out, forward_out, *rest,
):
    *send_outs, send, scratch = rest
    heads, parts, rows, columns, terms = chunk_of(
        key, value, gate, beta, rims.at[1], rims.at[2], key_taps, value_taps, scratch
    )
    carries, moves = [], []
    for i, (at, decay, summary, solved, forward) in enumerate(zip(parts, *terms)):
        solved_out[i] = solved
        forward_out[:, at] = forward.astype(forward_out.dtype)
        steady = jnp.where(rows == columns, decay, 0.0)
        carry = jnp.concatenate([steady - summary[:DK], summary[DK:]], axis=0)
        carry_out[i] = carry.astype(BF16)
        carries.append(carry)
    for i, carry in enumerate(carries):
        moves.append(mm(carry, later_summary[i, :DK, :], NN, PASS_COMP))
    for head, decay, summary, moved in zip(heads, terms[0], terms[1], moves):
        after = later_decay[head, 0:1, :]
        product = summary[:DK] * after + moved[:DK]
        offset = summary[DK:] * after - moved[DK:] + later_summary[head, DK:, :]
        both = decay * after
        high = both.astype(BF16)
        low = (both - high.astype(F32)).astype(BF16)
        slot = lax.bitwise_xor(head, where[0])
        send[slot, 0:DK, :] = product.astype(BF16)
        send[slot, DK : 2 * DK, :] = offset.astype(BF16)
        send[slot, 2 * DK : 2 * DK + 16, :] = jnp.concatenate(
            [jnp.broadcast_to(high, (8, DK)), jnp.broadcast_to(low, (8, DK))], axis=0
        )
    for slot, out in enumerate(send_outs):
        out[...] = send[slot]


def output_kernel(
    first_head, query, gate, rims, query_taps,
    first_solved, later_solved, first_forward, later_forward, carry, matrix,
    direct_out, coefficient_out, *rest,
):
    *kept, scratch = rest
    if kept:
        matrix_out, arrived = kept
        fetch = pltpu.make_async_copy(matrix, matrix_out, arrived)
        fetch.start()
    step_heads = query.shape[1] // DK
    query_rim = rims[0, :, first_head * DK : first_head * DK + query.shape[1]]
    rows, columns = iotas()
    queries_all = conv_silu(scratch, query[...], query_rim[8:16, :], query_taps)
    units = [(i, c) for i in range(step_heads) for c in range(2)]
    wide = [slice(i * DK, (i + 1) * DK) for i, _ in units]
    tall = [slice(c * CHUNK, (c + 1) * CHUNK) for _, c in units]
    solved = [(first_solved, later_solved)[c][first_head + i] for i, c in units]
    forward = [
        (first_forward, later_forward)[c][:, (first_head + i) * DK : (first_head + i + 1) * DK]
        for i, c in units
    ]
    cumul = [cumulate(gate[t, w], rows, columns) for t, w in zip(tall, wide)]
    middle = [c[MID : MID + 1, :] for c in cumul]
    queries = [normalize(queries_all[t, w]) * DK ** (-0.5) for t, w in zip(tall, wide)]
    queried = [q * jnp.exp(c - m) for q, c, m in zip(queries, cumul, middle)]
    scores = [mm(q, f, NT, PASS_SCORES) for q, f in zip(queried, forward)]
    scores = [jnp.where(columns <= rows, x, 0.0) for x in scores]
    moved = [mm(x, u, NN, PASS_SU) for x, u in zip(scores, solved)]
    weights = [
        (q * jnp.exp(m) - x[:, :DK]).astype(BF16) for q, m, x in zip(queried, middle, moved)
    ]
    later = [
        dot(w, carry[first_head + i], NT) if c == 1 else None for (i, c), w in zip(units, weights)
    ]
    for (i, c), t, w, weight, x, extra in zip(units, tall, wide, weights, moved, later):
        direct = x[:, DK:]
        if c == 1:
            direct = direct + extra[:, DK:]
            weight = extra[:, :DK].astype(BF16)
        direct_out[t, w] = direct
        coefficient_out[t, w] = weight
    if kept:
        fetch.wait()


def scan_kernel(count, where, *refs):
    tables, (states_out, table) = refs[:count], refs[count:]
    for slot in range(count):
        table[slot] = tables[slot][...]
    state = jnp.zeros((DK, DK), F32)
    for shard in range(count):
        slot = lax.bitwise_xor(where[0], shard)
        states_out[slot] = state.astype(BF16)
        if shard < count - 1:
            high = table[slot, 2 * DK : 2 * DK + 1, :].astype(F32)
            low = table[slot, 2 * DK + 8 : 2 * DK + 9, :].astype(F32)
            state = (
                state * (high + low)
                - dot(state.astype(BF16), table[slot, 0:DK, :], NN)
                + table[slot, DK : 2 * DK, :].astype(F32)
            )


def tail_kernel(query, key, value, out):
    out[0] = query[...]
    out[1] = key[...]
    out[2] = value[...]


def project_kernel(heads, owners, where, mine, direct_one, direct_two, weight_one, weight_two, matrix, states, *rest):
    *outs, head_out, ordered = rest
    parts = len(owners)
    share = head_out.shape[0] // parts

    @pl.when(pl.program_id(0) == 0)
    def _():
        for head in range(heads):
            at = slice(head * DK, (head + 1) * DK)
            half, inner = divmod(head, heads // 2)
            near = slice(inner * DK, (inner + 1) * DK)
            slot = lax.bitwise_xor(where[0], head)
            total = (direct_one, direct_two)[half][:, near] + dot(
                (weight_one, weight_two)[half][:, near], states[slot], NT
            )
            head_out[:, at] = total.astype(BF16)
        for distance in range(parts):
            owner = owners[distance](mine[0])
            ordered[distance * share : (distance + 1) * share, :] = head_out[
                pl.ds(pl.multiple_of(owner * share, share), share), :
            ]

    total = dot(ordered[...], matrix[...], NN)
    for distance in range(parts):
        outs[distance][...] = total[distance * share : (distance + 1) * share, :].astype(
            outs[distance].dtype
        )


def spec(shape, index):
    return pl.BlockSpec(shape, index)


def call(kernel, grid, in_specs, out_specs, out_shape, scratch, cost, limit, scalars, *args):
    return pl.pallas_call(
        kernel,
        grid_spec=pltpu.PrefetchScalarGridSpec(
            num_scalar_prefetch=scalars,
            grid=grid,
            in_specs=in_specs,
            out_specs=out_specs,
            scratch_shapes=scratch,
        ),
        out_shape=out_shape,
        compiler_params=pltpu.CompilerParams(
            dimension_semantics=("arbitrary",) * len(grid), vmem_limit_bytes=limit << 20
        ),
        cost_estimate=pl.CostEstimate(flops=cost[0], bytes_accessed=cost[1], transcendentals=0),
    )(*args)


def shards(query, key_in, value, gates, beta, conv_query, conv_key, conv_value, out_weight):
    length, width = query.shape
    groups = beta.shape[1]
    taps = conv_query.shape[0]
    ranks = lax.axis_size("seq")
    me = lax.axis_index("seq").astype(jnp.int32)
    spread = groups == ranks
    order = me if spread else jnp.zeros((), jnp.int32)
    shape = jax.ShapeDtypeStruct
    kept = pltpu.VMEM
    here = pl.BlockSpec(memory_space=pltpu.VMEM)
    query, key_in, value, gates, beta_rows, conv_query, conv_key, conv_value, out_weight = (
        pltpu.with_memory_space_constraint(data, pltpu.HBM)
        for data in (
            query, key_in, value, gates, beta.T, conv_query, conv_key, conv_value, out_weight
        )
    )
    tail_spec = spec((HALO, width), lambda p: (length // HALO - 1, 0))
    rims = call(
        tail_kernel, (1,), [tail_spec] * 3,
        spec((3, HALO, width), lambda p: (0, 0, 0)), shape((3, HALO, width), BF16),
        [], (0, 3 * HALO * width * 4), LIMIT, 0, query, key_in, value,
    )
    rims = lax.ppermute(rims, "seq", [(i, i + 1) for i in range(ranks - 1)])

    def chunk_specs(c):
        return [spec((CHUNK, width), lambda p, *_: (c, 0))] * 3 + [
            spec((groups, CHUNK), lambda p, *_: (0, c))
        ]

    tap_spec = spec((taps, width), lambda p, *_: (0, 0))
    rim_spec = spec((HALO, width), lambda p, *_: (CHUNK // HALO - 1, 0))
    solved_shape = kept((groups, CHUNK, 2 * DK), F32)
    forward_shape = kept((CHUNK, width), BF16 if PASS_SCORES == 1 else F32)
    conv_scratch = pltpu.VMEM((2, 8 + CHUNK, width), F32)
    cost = (groups * 100_000_000, 4 << 20)

    later_summary, later_decay, later_solved, later_forward = call(
        later_kernel,
        (1,),
        chunk_specs(1) + [rim_spec, rim_spec, tap_spec, tap_spec],
        [here] * 4,
        [kept((groups, 2 * DK, DK), F32), kept((groups, 8, DK), F32), solved_shape, forward_shape],
        [conv_scratch],
        cost,
        LIMIT,
        0,
        key_in, value, gates, beta_rows, key_in, value, conv_key, conv_value,
    )
    packed = 2 * DK + 16
    carry, first_solved, first_forward, *send = call(
        first_kernel,
        (1,),
        chunk_specs(0) + [here, tap_spec, tap_spec, here, here],
        [here] * (3 + groups),
        [kept((groups, 2 * DK, DK), BF16), solved_shape, forward_shape]
        + [kept((packed, DK), BF16)] * groups,
        [pltpu.VMEM((groups, packed, DK), BF16), conv_scratch],
        cost,
        LIMIT,
        1,
        order[None], key_in, value, gates, beta_rows, rims, conv_key, conv_value,
        later_summary, later_decay,
    )

    def exchange(blocks):
        return [blocks[0]] + [
            lax.ppermute(blocks[m], "seq", [(i, i ^ m) for i in range(ranks)])
            for m in range(1, ranks)
        ]

    def outputs(half, later_solved, fetch):
        half_spec = spec((length, width // 2), lambda p: (0, half))
        extra_shape = [kept(out_weight.shape, BF16)] if fetch else []
        return call(
            functools.partial(output_kernel, half * groups // 2),
            (1,),
            [half_spec, half_spec, here, spec((taps, width // 2), lambda p: (0, half))]
            + [here] * 5
            + [pl.BlockSpec(memory_space=pl.ANY)],
            [here] * (3 if fetch else 2),
            [kept((length, width // 2), F32), kept((length, width // 2), BF16)] + extra_shape,
            ([pltpu.SemaphoreType.DMA] if fetch else [])
            + [pltpu.VMEM((8 + length, width // 2), F32)],
            (groups * 50_000_000, 2 << 20),
            LIMIT,
            0,
            query, gates, rims, conv_query,
            first_solved, later_solved, first_forward, later_forward, carry, out_weight,
        )

    direct_one, weight_one, matrix = outputs(0, later_solved, True)
    if spread:
        arrived = exchange(send)
        arrived, direct_one, weight_one, matrix = lax.optimization_barrier((arrived, direct_one, weight_one, matrix))
        states = call(
            functools.partial(scan_kernel, ranks),
            (1,),
            [here] * ranks,
            spec((ranks, DK, DK), lambda p, *_: (0, 0, 0)),
            shape((ranks, DK, DK), BF16),
            [pltpu.VMEM((ranks, packed, DK), BF16)],
            (ranks * 4_000_000, 1 << 20),
            LIMIT,
            1,
            me[None], *arrived,
        )
        states, later_solved = lax.optimization_barrier((states, later_solved))
        direct_two, weight_two = outputs(1, later_solved, False)
        states = jnp.stack(exchange(states))
        states, direct_two, weight_two, matrix = lax.optimization_barrier(
            (states, direct_two, weight_two, matrix)
        )
    else:
        direct_two, weight_two = outputs(1, later_solved, False)
        every = lax.all_gather(jnp.stack(send), "seq")
        product, offset = every[:, :, :DK].astype(F32), every[:, :, DK : 2 * DK].astype(F32)
        decay = every[:, :, 2 * DK : 2 * DK + 1].astype(F32) + every[:, :, 2 * DK + 8 : 2 * DK + 9].astype(F32)
        state = jnp.zeros((groups, DK, DK), F32)
        states = state
        for shard in range(ranks):
            states = jnp.where(me == shard, state, states)
            moved = jnp.einsum("hij,hjk->hik", state, product[shard], precision=lax.Precision.HIGHEST)
            state = state * decay[shard] - moved + offset[shard]
        states = states.astype(BF16)

    parts = lax.axis_size("head")
    mine = lax.axis_index("head").astype(jnp.int32)
    share = length // parts
    model = out_weight.shape[1]
    if parts == 4:
        owners = (
            lambda z: z,
            lambda z: jnp.where(lax.rem(z, 2) == 0, 3, 0),
            lambda z: jnp.where(z < 2, 2, 1),
            lambda z: lax.rem(2 * z + 1, 5),
        )
    else:
        owners = [lambda z, d=d: lax.rem(z + d, parts) for d in range(parts)]
    own, *leaving = call(
        functools.partial(project_kernel, groups, owners),
        (1,),
        [here] * 5 + [spec((groups, DK, DK), lambda p, *_: (0, 0, 0))],
        [here] * parts,
        [kept((share, model), F32)] + [kept((share, model), BF16)] * (parts - 1),
        [pltpu.VMEM((length, width), BF16)] * 2,
        (2 * length * width * model, width * model * 2),
        LIMIT,
        2,
        order[None], mine[None], direct_one, direct_two, weight_one, weight_two, matrix, states,
    )
    if parts == 4:
        near, inward, last = leaving
        middle = (mine == 1) | (mine == 2)
        near = lax.ppermute(near, "head", [(0, 1), (1, 0), (2, 3), (3, 2)]).astype(F32)
        skipped = lax.ppermute(inward, "head", [(0, 2), (3, 1)])
        crossed = lax.ppermute(inward, "head", [(1, 2), (2, 1)])
        joined = (last.astype(F32) + jnp.where(middle, near, 0.0)).astype(BF16)
        joined = lax.ppermute(joined, "head", [(0, 1), (3, 2), (1, 3), (2, 0)])
        arrived = [jnp.where(middle, 0.0, near), skipped, crossed, joined]
    else:
        arrived = [
            lax.ppermute(part, "head", [(i, (i + d) % parts) for i in range(parts)])
            for d, part in enumerate(leaving, 1)
        ]
    total = own
    for part in arrived:
        total = total + part.astype(F32)
    return total.astype(BF16)


def solution(mesh):
    in_specs = (
        P("seq", "head"),
        P("seq", "head"),
        P("seq", "head"),
        P("seq", "head"),
        P("seq", "head"),
        P(None, "head"),
        P(None, "head"),
        P(None, "head"),
        P("head", None),
    )
    out_specs = P(("seq", "head"), None)
    return jax.shard_map(shards, mesh=mesh, in_specs=in_specs, out_specs=out_specs, check_vma=False)
```

```python
import functools

import jax
import jax.numpy as jnp
from jax import lax
from jax.experimental import pallas as pl
from jax.experimental.pallas import tpu as pltpu
from jax.sharding import PartitionSpec as P

DK = 128
CHUNK = 128
MID = 63
HALO = 16
BASE = 16
LIMIT = 32
F32 = jnp.float32
BF16 = jnp.bfloat16

PASS_A = 3
PASS_SOLVE = 3
PASS_UW = 3
PASS_PO = 3
PASS_COMP = 2
PASS_SCORES = 1
PASS_SU = 3

NN = (((1,), (0,)), ((), ()))
NT = (((1,), (1,)), ((), ()))
TN = (((0,), (0,)), ((), ()))


def dot(left, right, dims):
    return lax.dot_general(left, right, dims, preferred_element_type=F32)


def split(data):
    high = data.astype(BF16)
    return high, (data - high.astype(F32)).astype(BF16)


def mm(left, right, dims, passes):
    if passes == 1:
        return dot(left.astype(BF16), right.astype(BF16), dims)
    left_high, left_low = split(left)
    if passes == 2:
        right = right.astype(BF16)
        return dot(left_high, right, dims) + dot(left_low, right, dims)
    right_high, right_low = split(right)
    return dot(left_high, right_high, dims) + (
        dot(left_low, right_high, dims) + dot(left_high, right_low, dims)
    )


def conv_silu(scratch, data, before, taps):
    count, width = data.shape
    scratch[0:8, :] = before.astype(F32)
    scratch[8 : 8 + count, :] = data.astype(F32)
    number = taps.shape[0]
    total = taps[number - 1 : number, :].astype(F32) * scratch[8 : 8 + count, :]
    for tap in range(number - 1):
        first = 8 - (number - 1) + tap
        total = total + taps[tap : tap + 1, :].astype(F32) * scratch[first : first + count, :]
    return total / (1.0 + jnp.exp(-total))


def normalize(data):
    return data * lax.rsqrt(jnp.sum(data * data, axis=-1, keepdims=True) + 1e-06)


def iotas():
    rows = lax.broadcasted_iota(jnp.int32, (CHUNK, CHUNK), 0)
    columns = lax.broadcasted_iota(jnp.int32, (CHUNK, CHUNK), 1)
    return rows, columns


def cumulate(gates, rows, columns):
    ones = jnp.where(columns <= rows, 1.0, 0.0).astype(BF16)
    return dot(ones, gates, NN)


def inverse_blocks(matrices, rows, columns):
    lanes = lax.broadcasted_iota(jnp.int32, (8, CHUNK), 1)
    inner = lax.broadcasted_iota(jnp.int32, (8, CHUNK), 0)
    tiles = BASE // 8
    packed, solved = [], []
    for matrix in matrices:
        pack = []
        for t in range(tiles):
            total = jnp.zeros((8, CHUNK), F32)
            for b in range(CHUNK // BASE):
                first = b * BASE + t * 8
                total = jnp.where(lanes // BASE == b, matrix[first : first + 8, :], total)
            pack.append(total)
        packed.append(pack)
        solved.append([jnp.where(lanes % BASE == inner + 8 * t, 1.0, 0.0) for t in range(tiles)])
    for j in range(BASE - 1):
        pick = (lanes // BASE) * BASE + j
        for pack, block in zip(packed, solved):
            row = jnp.broadcast_to(block[j // 8][j % 8 : j % 8 + 1, :], (8, CHUNK))
            for t in range(j // 8, tiles):
                factor = jnp.take_along_axis(pack[t], pick, axis=1)
                block[t] = block[t] - factor * row
    results = []
    for block in solved:
        tall = jnp.concatenate(block * (CHUNK // BASE), axis=0)
        results.append(jnp.where(rows // BASE == columns // BASE, tall, 0.0))
    size = BASE
    while size < CHUNK:
        here = (rows // (2 * size) == columns // (2 * size)) & (rows // size != columns // size)
        moved = [
            mm(jnp.where(here, matrix, 0.0), result, NN, PASS_SOLVE)
            for matrix, result in zip(matrices, results)
        ]
        results = [
            result - mm(result, move, NN, PASS_SOLVE) for result, move in zip(results, moved)
        ]
        size *= 2
    return results


def column_of(row, rows, columns):
    return jnp.sum(jnp.where(rows == columns, row, 0.0), axis=-1, keepdims=True)


def chunk_terms(keys, values, gates, betas, rows, columns):
    cumul = [cumulate(g, rows, columns) for g in gates]
    middle = [c[MID : MID + 1, :] for c in cumul]
    final = [c[CHUNK - 1 : CHUNK, :] for c in cumul]
    forward = [k * jnp.exp(m - c) for k, m, c in zip(keys, middle, cumul)]
    backward = [k * jnp.exp(c - m) for k, m, c in zip(keys, middle, cumul)]
    coupling = [mm(b, f, NT, PASS_A) for b, f in zip(backward, forward)]
    strict = [jnp.where(columns < rows, a * b, 0.0) for a, b in zip(coupling, betas)]
    solver = inverse_blocks(strict, rows, columns)
    sides = [
        jnp.concatenate([beta * b * jnp.exp(m), beta * v], axis=-1)
        for beta, b, m, v in zip(betas, backward, middle, values)
    ]
    solved = [mm(x, side, NN, PASS_UW) for x, side in zip(solver, sides)]
    trailing = [f * jnp.exp(e - m) for f, e, m in zip(forward, final, middle)]
    summary = [mm(u, t, TN, PASS_PO) for u, t in zip(solved, trailing)]
    return [jnp.exp(e) for e in final], summary, solved, forward


def chunk_of(key, value, gate, beta, key_rim, value_rim, key_taps, value_taps, scratch):
    rows, columns = iotas()
    keys_all = conv_silu(scratch.at[0], key[...], key_rim[8:16, :], key_taps)
    values_all = conv_silu(scratch.at[1], value[...], value_rim[8:16, :], value_taps)
    heads = range(beta.shape[0])
    parts = [slice(i * DK, (i + 1) * DK) for i in heads]
    terms = chunk_terms(
        [normalize(keys_all[:, at]) for at in parts],
        [values_all[:, at] for at in parts],
        [gate[:, at] for at in parts],
        [column_of(beta[i : i + 1, :], rows, columns) for i in heads],
        rows,
        columns,
    )
    return heads, parts, rows, columns, terms


def later_kernel(
    key, value, gate, beta, key_rim, value_rim, key_taps, value_taps,
    summary_out, decay_out, solved_out, forward_out, scratch,
):
    _, parts, _, _, terms = chunk_of(
        key, value, gate, beta, key_rim, value_rim, key_taps, value_taps, scratch
    )
    for i, (at, decay, summary, solved, forward) in enumerate(zip(parts, *terms)):
        summary_out[i] = summary
        decay_out[i] = jnp.broadcast_to(decay, (8, DK))
        solved_out[i] = solved
        forward_out[:, at] = forward.astype(forward_out.dtype)


def first_kernel(
    where, key, value, gate, beta, rims, key_taps, value_taps, later_summary, later_decay,
    carry_out, solved_out, forward_out, *rest,
):
    *send_outs, send, scratch = rest
    heads, parts, rows, columns, terms = chunk_of(
        key, value, gate, beta, rims.at[1], rims.at[2], key_taps, value_taps, scratch
    )
    carries, moves = [], []
    for i, (at, decay, summary, solved, forward) in enumerate(zip(parts, *terms)):
        solved_out[i] = solved
        forward_out[:, at] = forward.astype(forward_out.dtype)
        steady = jnp.where(rows == columns, decay, 0.0)
        carry = jnp.concatenate([steady - summary[:DK], summary[DK:]], axis=0)
        carry_out[i] = carry.astype(BF16)
        carries.append(carry)
    for i, carry in enumerate(carries):
        moves.append(mm(carry, later_summary[i, :DK, :], NN, PASS_COMP))
    for head, decay, summary, moved in zip(heads, terms[0], terms[1], moves):
        after = later_decay[head, 0:1, :]
        product = summary[:DK] * after + moved[:DK]
        offset = summary[DK:] * after - moved[DK:] + later_summary[head, DK:, :]
        both = decay * after
        high = both.astype(BF16)
        low = (both - high.astype(F32)).astype(BF16)
        slot = lax.bitwise_xor(head, where[0])
        send[slot, 0:DK, :] = product.astype(BF16)
        send[slot, DK : 2 * DK, :] = offset.astype(BF16)
        send[slot, 2 * DK : 2 * DK + 16, :] = jnp.concatenate(
            [jnp.broadcast_to(high, (8, DK)), jnp.broadcast_to(low, (8, DK))], axis=0
        )
    for slot, out in enumerate(send_outs):
        out[...] = send[slot]


def output_kernel(
    first_head, query, gate, rims, query_taps,
    first_solved, later_solved, first_forward, later_forward, carry, matrix,
    direct_out, coefficient_out, *rest,
):
    *kept, scratch = rest
    if kept:
        matrix_out, arrived = kept
        fetch = pltpu.make_async_copy(matrix, matrix_out, arrived)
        fetch.start()
    step_heads = query.shape[1] // DK
    query_rim = rims[0, :, first_head * DK : first_head * DK + query.shape[1]]
    rows, columns = iotas()
    queries_all = conv_silu(scratch, query[...], query_rim[8:16, :], query_taps)
    units = [(i, c) for i in range(step_heads) for c in range(2)]
    wide = [slice(i * DK, (i + 1) * DK) for i, _ in units]
    tall = [slice(c * CHUNK, (c + 1) * CHUNK) for _, c in units]
    solved = [(first_solved, later_solved)[c][first_head + i] for i, c in units]
    forward = [
        (first_forward, later_forward)[c][:, (first_head + i) * DK : (first_head + i + 1) * DK]
        for i, c in units
    ]
    cumul = [cumulate(gate[t, w], rows, columns) for t, w in zip(tall, wide)]
    middle = [c[MID : MID + 1, :] for c in cumul]
    queries = [normalize(queries_all[t, w]) * DK ** (-0.5) for t, w in zip(tall, wide)]
    queried = [q * jnp.exp(c - m) for q, c, m in zip(queries, cumul, middle)]
    scores = [mm(q, f, NT, PASS_SCORES) for q, f in zip(queried, forward)]
    scores = [jnp.where(columns <= rows, x, 0.0) for x in scores]
    moved = [mm(x, u, NN, PASS_SU) for x, u in zip(scores, solved)]
    weights = [
        (q * jnp.exp(m) - x[:, :DK]).astype(BF16) for q, m, x in zip(queried, middle, moved)
    ]
    later = [
        dot(w, carry[first_head + i], NT) if c == 1 else None for (i, c), w in zip(units, weights)
    ]
    for (i, c), t, w, weight, x, extra in zip(units, tall, wide, weights, moved, later):
        direct = x[:, DK:]
        if c == 1:
            direct = direct + extra[:, DK:]
            weight = extra[:, :DK].astype(BF16)
        direct_out[t, w] = direct
        coefficient_out[t, w] = weight
    if kept:
        fetch.wait()


def scan_kernel(count, where, *refs):
    tables, outs, (states, table) = refs[:count], refs[count:-2], refs[-2:]
    for slot in range(count):
        table[slot] = tables[slot][...]
    state = jnp.zeros((DK, DK), F32)
    for shard in range(count):
        slot = lax.bitwise_xor(where[0], shard)
        states[slot] = state.astype(BF16)
        if shard < count - 1:
            high = table[slot, 2 * DK : 2 * DK + 1, :].astype(F32)
            low = table[slot, 2 * DK + 8 : 2 * DK + 9, :].astype(F32)
            state = (
                state * (high + low)
                - dot(state.astype(BF16), table[slot, 0:DK, :], NN)
                + table[slot, DK : 2 * DK, :].astype(F32)
            )
    for pair, out in enumerate(outs):
        out[...] = states[2 * pair : 2 * pair + 2]


def fetch_kernel(source, out, arrived):
    copy = pltpu.make_async_copy(source.at[:, 0 : out.shape[1]], out, arrived)
    copy.start()
    copy.wait()


def gather_kernel(*refs):
    *pairs, out = refs
    for i, pair in enumerate(pairs):
        out[i] = pair[1]


def tail_kernel(query, key, value, out):
    out[0] = query[...]
    out[1] = key[...]
    out[2] = value[...]


def project_kernel(heads, owners, where, mine, direct_one, direct_two, weight_one, weight_two, early, matrix, *rest):
    arrived, rest = rest[: heads // 2 + 1], rest[heads // 2 + 1 :]
    *outs, head_out, ordered, states, late, landed = rest
    half_width = early.shape[1]
    copy = pltpu.make_async_copy(matrix.at[:, half_width:], late, landed)
    copy.start()
    for pair in range(heads // 2):
        states[2 * pair] = arrived[pair][0]
        states[2 * pair + 1] = arrived[-1][pair]
    parts = len(owners)
    share = head_out.shape[0] // parts

    @pl.when(pl.program_id(0) == 0)
    def _():
        for head in range(heads):
            at = slice(head * DK, (head + 1) * DK)
            half, inner = divmod(head, heads // 2)
            near = slice(inner * DK, (inner + 1) * DK)
            slot = lax.bitwise_xor(where[0], head)
            total = (direct_one, direct_two)[half][:, near] + dot(
                (weight_one, weight_two)[half][:, near], states[slot], NT
            )
            head_out[:, at] = total.astype(BF16)
        for distance in range(parts):
            owner = owners[distance](mine[0])
            ordered[distance * share : (distance + 1) * share, :] = head_out[
                pl.ds(pl.multiple_of(owner * share, share), share), :
            ]

    for side in range(2):
        if side == 1:
            copy.wait()
        total = dot(ordered[...], (early, late)[side][...], NN)
        at = slice(side * half_width, side * half_width + total.shape[1])
        for distance in range(parts):
            outs[distance][:, at] = total[distance * share : (distance + 1) * share, :].astype(
                outs[distance].dtype
            )


def spec(shape, index):
    return pl.BlockSpec(shape, index)


def call(kernel, grid, in_specs, out_specs, out_shape, scratch, cost, limit, scalars, *args):
    return pl.pallas_call(
        kernel,
        grid_spec=pltpu.PrefetchScalarGridSpec(
            num_scalar_prefetch=scalars,
            grid=grid,
            in_specs=in_specs,
            out_specs=out_specs,
            scratch_shapes=scratch,
        ),
        out_shape=out_shape,
        compiler_params=pltpu.CompilerParams(
            dimension_semantics=("arbitrary",) * len(grid), vmem_limit_bytes=limit << 20
        ),
        cost_estimate=pl.CostEstimate(flops=cost[0], bytes_accessed=cost[1], transcendentals=0),
    )(*args)


def shards(query, key_in, value, gates, beta, conv_query, conv_key, conv_value, out_weight):
    length, width = query.shape
    groups = beta.shape[1]
    taps = conv_query.shape[0]
    ranks = lax.axis_size("seq")
    me = lax.axis_index("seq").astype(jnp.int32)
    spread = groups == ranks
    order = me if spread else jnp.zeros((), jnp.int32)
    shape = jax.ShapeDtypeStruct
    kept = pltpu.VMEM
    here = pl.BlockSpec(memory_space=pltpu.VMEM)
    anywhere = pl.BlockSpec(memory_space=pl.ANY)
    query, key_in, value, gates, beta_rows, conv_query, conv_key, conv_value, out_weight = (
        pltpu.with_memory_space_constraint(data, pltpu.HBM)
        for data in (
            query, key_in, value, gates, beta.T, conv_query, conv_key, conv_value, out_weight
        )
    )
    tail_spec = spec((HALO, width), lambda p: (length // HALO - 1, 0))
    rims = call(
        tail_kernel, (1,), [tail_spec] * 3,
        spec((3, HALO, width), lambda p: (0, 0, 0)), shape((3, HALO, width), BF16),
        [], (0, 3 * HALO * width * 4), LIMIT, 0, query, key_in, value,
    )
    rims = lax.ppermute(rims, "seq", [(i, i + 1) for i in range(ranks - 1)])

    def chunk_specs(c):
        return [spec((CHUNK, width), lambda p, *_: (c, 0))] * 3 + [
            spec((groups, CHUNK), lambda p, *_: (0, c))
        ]

    tap_spec = spec((taps, width), lambda p, *_: (0, 0))
    rim_spec = spec((HALO, width), lambda p, *_: (CHUNK // HALO - 1, 0))
    solved_shape = kept((groups, CHUNK, 2 * DK), F32)
    forward_shape = kept((CHUNK, width), BF16 if PASS_SCORES == 1 else F32)
    conv_scratch = pltpu.VMEM((2, 8 + CHUNK, width), F32)
    cost = (groups * 100_000_000, 4 << 20)

    later_summary, later_decay, later_solved, later_forward = call(
        later_kernel,
        (1,),
        chunk_specs(1) + [rim_spec, rim_spec, tap_spec, tap_spec],
        [here] * 4,
        [kept((groups, 2 * DK, DK), F32), kept((groups, 8, DK), F32), solved_shape, forward_shape],
        [conv_scratch],
        cost,
        LIMIT,
        0,
        key_in, value, gates, beta_rows, key_in, value, conv_key, conv_value,
    )
    packed = 2 * DK + 16
    carry, first_solved, first_forward, *send = call(
        first_kernel,
        (1,),
        chunk_specs(0) + [here, tap_spec, tap_spec, here, here],
        [here] * (3 + groups),
        [kept((groups, 2 * DK, DK), BF16), solved_shape, forward_shape]
        + [kept((packed, DK), BF16)] * groups,
        [pltpu.VMEM((groups, packed, DK), BF16), conv_scratch],
        cost,
        LIMIT,
        1,
        order[None], key_in, value, gates, beta_rows, rims, conv_key, conv_value,
        later_summary, later_decay,
    )

    def exchange(blocks):
        return [blocks[0]] + [
            lax.ppermute(blocks[m], "seq", [(i, i ^ m) for i in range(ranks)])
            for m in range(1, ranks)
        ]

    def outputs(half, later_solved, fetch):
        half_spec = spec((length, width // 2), lambda p: (0, half))
        extra_shape = [kept(out_weight.shape, BF16)] if fetch else []
        return call(
            functools.partial(output_kernel, half * groups // 2),
            (1,),
            [half_spec, half_spec, here, spec((taps, width // 2), lambda p: (0, half))]
            + [here] * 5
            + [pl.BlockSpec(memory_space=pl.ANY)],
            [here] * (3 if fetch else 2),
            [kept((length, width // 2), F32), kept((length, width // 2), BF16)] + extra_shape,
            ([pltpu.SemaphoreType.DMA] if fetch else [])
            + [pltpu.VMEM((8 + length, width // 2), F32)],
            (groups * 50_000_000, 2 << 20),
            LIMIT,
            0,
            query, gates, rims, conv_query,
            first_solved, later_solved, first_forward, later_forward, carry, out_weight,
        )

    direct_one, weight_one = outputs(0, later_solved, False)
    if spread:
        arrived = exchange(send)
        arrived, direct_one, weight_one = lax.optimization_barrier((arrived, direct_one, weight_one))
        states = call(
            functools.partial(scan_kernel, ranks),
            (1,),
            [here] * ranks,
            [here] * (ranks // 2),
            [shape((2, DK, DK), BF16)] * (ranks // 2),
            [pltpu.VMEM((ranks, DK, DK), BF16), pltpu.VMEM((ranks, packed, DK), BF16)],
            (ranks * 4_000_000, 1 << 20),
            LIMIT,
            1,
            me[None], *arrived,
        )
        states, later_solved = lax.optimization_barrier((states, later_solved))
        direct_two, weight_two = outputs(1, later_solved, False)
        states = [states[0]] + [
            lax.ppermute(states[d], "seq", [(i, i ^ (2 * d)) for i in range(ranks)])
            for d in range(1, ranks // 2)
        ]
        states, direct_two, weight_two = lax.optimization_barrier((states, direct_two, weight_two))
        aside = call(
            gather_kernel, (1,), [here] * (ranks // 2), here,
            shape((ranks // 2, DK, DK), BF16), [], (0, 1 << 18), LIMIT, 0, *states,
        )
        aside, source = lax.optimization_barrier((aside, out_weight))
        states = states + [lax.ppermute(aside, "seq", [(i, i ^ 1) for i in range(ranks)])]
    else:
        direct_two, weight_two = outputs(1, later_solved, False)
        every = lax.all_gather(jnp.stack(send), "seq")
        product, offset = every[:, :, :DK].astype(F32), every[:, :, DK : 2 * DK].astype(F32)
        decay = every[:, :, 2 * DK : 2 * DK + 1].astype(F32) + every[:, :, 2 * DK + 8 : 2 * DK + 9].astype(F32)
        state = jnp.zeros((groups, DK, DK), F32)
        states = state
        for shard in range(ranks):
            states = jnp.where(me == shard, state, states)
            moved = jnp.einsum("hij,hjk->hik", state, product[shard], precision=lax.Precision.HIGHEST)
            state = state * decay[shard] - moved + offset[shard]
        states = states.astype(BF16)
        source = out_weight
        states = [states[i : i + 2] for i in range(0, groups, 2)] + [states[1::2]]

    parts = lax.axis_size("head")
    mine = lax.axis_index("head").astype(jnp.int32)
    share = length // parts
    model = out_weight.shape[1]
    if parts == 4:
        owners = (
            lambda z: z,
            lambda z: jnp.where(lax.rem(z, 2) == 0, 3, 0),
            lambda z: jnp.where(z < 2, 2, 1),
            lambda z: lax.rem(2 * z + 1, 5),
        )
    else:
        owners = [lambda z, d=d: lax.rem(z + d, parts) for d in range(parts)]
    half = model // 2
    early = call(
        fetch_kernel, (1,), [anywhere], here, kept((width, half), BF16),
        [pltpu.SemaphoreType.DMA], (0, width * model * 2), LIMIT, 0, source,
    )
    own, *leaving = call(
        functools.partial(project_kernel, groups, owners),
        (1,),
        [here] * 5 + [anywhere] + [here] * (groups // 2 + 1),
        [here] * parts,
        [kept((share, model), F32)] + [kept((share, model), BF16)] * (parts - 1),
        [pltpu.VMEM((length, width), BF16)] * 2
        + [
            pltpu.VMEM((groups, DK, DK), BF16),
            pltpu.VMEM((width, model - half), BF16),
            pltpu.SemaphoreType.DMA,
        ],
        (2 * length * width * model, width * model * 2),
        LIMIT,
        2,
        order[None], mine[None], direct_one, direct_two, weight_one, weight_two, early, source, *states,
    )
    if parts == 4:
        near, inward, last = leaving
        middle = (mine == 1) | (mine == 2)
        near = lax.ppermute(near, "head", [(0, 1), (1, 0), (2, 3), (3, 2)]).astype(F32)
        crossed = lax.ppermute(inward, "head", [(1, 2), (2, 1)])
        skipped = lax.ppermute(inward, "head", [(0, 2), (3, 1)])
        joined = (last.astype(F32) + jnp.where(middle, near, 0.0)).astype(BF16)
        joined = lax.ppermute(joined, "head", [(0, 1), (3, 2), (1, 3), (2, 0)])
        arrived = [jnp.where(middle, 0.0, near), crossed, skipped, joined]
    else:
        arrived = [
            lax.ppermute(part, "head", [(i, (i + d) % parts) for i in range(parts)])
            for d, part in enumerate(leaving, 1)
        ]
    total = own
    for part in arrived:
        total = total + part.astype(F32)
    return total.astype(BF16)


def solution(mesh):
    in_specs = (
        P("seq", "head"),
        P("seq", "head"),
        P("seq", "head"),
        P("seq", "head"),
        P("seq", "head"),
        P(None, "head"),
        P(None, "head"),
        P(None, "head"),
        P("head", None),
    )
    out_specs = P(("seq", "head"), None)
    return jax.shard_map(shards, mesh=mesh, in_specs=in_specs, out_specs=out_specs, check_vma=False)
```

```python
import functools

import jax
import jax.numpy as jnp
from jax import lax
from jax.experimental import pallas as pl
from jax.experimental.pallas import tpu as pltpu
from jax.sharding import PartitionSpec as P

DK = 128
CHUNK = 128
MID = 63
HALO = 16
BASE = 16
LIMIT = 32
F32 = jnp.float32
BF16 = jnp.bfloat16

PASS_A = 3
PASS_SOLVE = 3
PASS_UW = 3
PASS_PO = 3
PASS_COMP = 2
PASS_SCORES = 1
PASS_SU = 3

NN = (((1,), (0,)), ((), ()))
NT = (((1,), (1,)), ((), ()))
TN = (((0,), (0,)), ((), ()))


def dot(left, right, dims):
    return lax.dot_general(left, right, dims, preferred_element_type=F32)


def split(data):
    high = data.astype(BF16)
    return high, (data - high.astype(F32)).astype(BF16)


def mm(left, right, dims, passes):
    if passes == 1:
        return dot(left.astype(BF16), right.astype(BF16), dims)
    left_high, left_low = split(left)
    if passes == 2:
        right = right.astype(BF16)
        return dot(left_high, right, dims) + dot(left_low, right, dims)
    right_high, right_low = split(right)
    return dot(left_high, right_high, dims) + (
        dot(left_low, right_high, dims) + dot(left_high, right_low, dims)
    )


def conv_silu(scratch, data, before, taps):
    count, width = data.shape
    scratch[0:8, :] = before.astype(F32)
    scratch[8 : 8 + count, :] = data.astype(F32)
    number = taps.shape[0]
    total = taps[number - 1 : number, :].astype(F32) * scratch[8 : 8 + count, :]
    for tap in range(number - 1):
        first = 8 - (number - 1) + tap
        total = total + taps[tap : tap + 1, :].astype(F32) * scratch[first : first + count, :]
    return total * lax.logistic(total)


def normalize(data):
    return data * lax.rsqrt(jnp.sum(data * data, axis=-1, keepdims=True) + 1e-06)


def iotas():
    rows = lax.broadcasted_iota(jnp.int32, (CHUNK, CHUNK), 0)
    columns = lax.broadcasted_iota(jnp.int32, (CHUNK, CHUNK), 1)
    return rows, columns


def cumulate(gates, rows, columns):
    ones = jnp.where(columns <= rows, 1.0, 0.0).astype(BF16)
    return dot(ones, gates, NN)


def inverse_blocks(matrices, rows, columns):
    lanes = lax.broadcasted_iota(jnp.int32, (8, CHUNK), 1)
    inner = lax.broadcasted_iota(jnp.int32, (8, CHUNK), 0)
    tiles = BASE // 8
    packed, solved = [], []
    for matrix in matrices:
        pack = []
        for t in range(tiles):
            total = jnp.zeros((8, CHUNK), F32)
            for b in range(CHUNK // BASE):
                first = b * BASE + t * 8
                total = jnp.where(lanes // BASE == b, matrix[first : first + 8, :], total)
            pack.append(total)
        packed.append(pack)
        solved.append([jnp.where(lanes % BASE == inner + 8 * t, 1.0, 0.0) for t in range(tiles)])
    for j in range(BASE - 1):
        pick = (lanes // BASE) * BASE + j
        for pack, block in zip(packed, solved):
            row = jnp.broadcast_to(block[j // 8][j % 8 : j % 8 + 1, :], (8, CHUNK))
            for t in range(j // 8, tiles):
                factor = jnp.take_along_axis(pack[t], pick, axis=1)
                block[t] = block[t] - factor * row
    results = []
    for block in solved:
        tall = jnp.concatenate(block * (CHUNK // BASE), axis=0)
        results.append(jnp.where(rows // BASE == columns // BASE, tall, 0.0))
    size = BASE
    while size < CHUNK:
        here = (rows // (2 * size) == columns // (2 * size)) & (rows // size != columns // size)
        moved = [
            mm(jnp.where(here, matrix, 0.0), result, NN, PASS_SOLVE)
            for matrix, result in zip(matrices, results)
        ]
        results = [
            result - mm(result, move, NN, PASS_SOLVE) for result, move in zip(results, moved)
        ]
        size *= 2
    return results


def column_of(row, rows, columns):
    return jnp.sum(jnp.where(rows == columns, row, 0.0), axis=-1, keepdims=True)


def chunk_terms(keys, values, gates, betas, rows, columns):
    cumul = [cumulate(g, rows, columns) for g in gates]
    middle = [c[MID : MID + 1, :] for c in cumul]
    final = [c[CHUNK - 1 : CHUNK, :] for c in cumul]
    forward = [k * jnp.exp(m - c) for k, m, c in zip(keys, middle, cumul)]
    backward = [k * jnp.exp(c - m) for k, m, c in zip(keys, middle, cumul)]
    coupling = [mm(b, f, NT, PASS_A) for b, f in zip(backward, forward)]
    strict = [jnp.where(columns < rows, a * b, 0.0) for a, b in zip(coupling, betas)]
    solver = inverse_blocks(strict, rows, columns)
    sides = [
        jnp.concatenate([beta * b * jnp.exp(m), beta * v], axis=-1)
        for beta, b, m, v in zip(betas, backward, middle, values)
    ]
    solved = [mm(x, side, NN, PASS_UW) for x, side in zip(solver, sides)]
    trailing = [f * jnp.exp(e - m) for f, e, m in zip(forward, final, middle)]
    summary = [mm(u, t, TN, PASS_PO) for u, t in zip(solved, trailing)]
    return [jnp.exp(e) for e in final], summary, solved, forward


def chunk_of(key, value, gate, beta, key_rim, value_rim, key_taps, value_taps, scratch):
    rows, columns = iotas()
    keys_all = conv_silu(scratch.at[0], key[...], key_rim[8:16, :], key_taps)
    values_all = conv_silu(scratch.at[1], value[...], value_rim[8:16, :], value_taps)
    heads = range(beta.shape[0])
    parts = [slice(i * DK, (i + 1) * DK) for i in heads]
    terms = chunk_terms(
        [normalize(keys_all[:, at]) for at in parts],
        [values_all[:, at] for at in parts],
        [gate[:, at] for at in parts],
        [column_of(beta[i : i + 1, :], rows, columns) for i in heads],
        rows,
        columns,
    )
    return heads, parts, rows, columns, terms


def later_kernel(
    key, value, gate, beta, key_rim, value_rim, key_taps, value_taps,
    summary_out, decay_out, solved_out, forward_out, scratch,
):
    _, parts, _, _, terms = chunk_of(
        key, value, gate, beta, key_rim, value_rim, key_taps, value_taps, scratch
    )
    for i, (at, decay, summary, solved, forward) in enumerate(zip(parts, *terms)):
        summary_out[i] = summary
        decay_out[i] = jnp.broadcast_to(decay, (8, DK))
        solved_out[i] = solved
        forward_out[:, at] = forward.astype(forward_out.dtype)


def first_kernel(
    where, key, value, gate, beta, rims, key_taps, value_taps, later_summary, later_decay,
    carry_out, solved_out, forward_out, *rest,
):
    *send_outs, send, scratch = rest
    heads, parts, rows, columns, terms = chunk_of(
        key, value, gate, beta, rims.at[1], rims.at[2], key_taps, value_taps, scratch
    )
    carries, moves = [], []
    for i, (at, decay, summary, solved, forward) in enumerate(zip(parts, *terms)):
        solved_out[i] = solved
        forward_out[:, at] = forward.astype(forward_out.dtype)
        steady = jnp.where(rows == columns, decay, 0.0)
        carry = jnp.concatenate([steady - summary[:DK], summary[DK:]], axis=0)
        carry_out[i] = carry.astype(BF16)
        carries.append(carry)
    for i, carry in enumerate(carries):
        moves.append(mm(carry, later_summary[i, :DK, :], NN, PASS_COMP))
    for head, decay, summary, moved in zip(heads, terms[0], terms[1], moves):
        after = later_decay[head, 0:1, :]
        product = summary[:DK] * after + moved[:DK]
        offset = summary[DK:] * after - moved[DK:] + later_summary[head, DK:, :]
        both = decay * after
        high = both.astype(BF16)
        low = (both - high.astype(F32)).astype(BF16)
        slot = lax.bitwise_xor(head, where[0])
        send[slot, 0:DK, :] = product.astype(BF16)
        send[slot, DK : 2 * DK, :] = offset.astype(BF16)
        send[slot, 2 * DK : 2 * DK + 16, :] = jnp.concatenate(
            [jnp.broadcast_to(high, (8, DK)), jnp.broadcast_to(low, (8, DK))], axis=0
        )
    for slot, out in enumerate(send_outs):
        out[...] = send[slot]


def output_kernel(
    first_head, query, gate, rims, query_taps,
    first_solved, later_solved, first_forward, later_forward, carry, matrix,
    direct_out, coefficient_out, *rest,
):
    *kept, scratch = rest
    if kept:
        matrix_out, arrived = kept
        fetch = pltpu.make_async_copy(matrix, matrix_out, arrived)
        fetch.start()
    step_heads = query.shape[1] // DK
    query_rim = rims[0, :, first_head * DK : first_head * DK + query.shape[1]]
    rows, columns = iotas()
    queries_all = conv_silu(scratch, query[...], query_rim[8:16, :], query_taps)
    units = [(i, c) for i in range(step_heads) for c in range(2)]
    wide = [slice(i * DK, (i + 1) * DK) for i, _ in units]
    tall = [slice(c * CHUNK, (c + 1) * CHUNK) for _, c in units]
    solved = [(first_solved, later_solved)[c][first_head + i] for i, c in units]
    forward = [
        (first_forward, later_forward)[c][:, (first_head + i) * DK : (first_head + i + 1) * DK]
        for i, c in units
    ]
    cumul = [cumulate(gate[t, w], rows, columns) for t, w in zip(tall, wide)]
    middle = [c[MID : MID + 1, :] for c in cumul]
    queries = [normalize(queries_all[t, w]) * DK ** (-0.5) for t, w in zip(tall, wide)]
    queried = [q * jnp.exp(c - m) for q, c, m in zip(queries, cumul, middle)]
    scores = [mm(q, f, NT, PASS_SCORES) for q, f in zip(queried, forward)]
    scores = [jnp.where(columns <= rows, x, 0.0) for x in scores]
    moved = [mm(x, u, NN, PASS_SU) for x, u in zip(scores, solved)]
    weights = [
        (q * jnp.exp(m) - x[:, :DK]).astype(BF16) for q, m, x in zip(queried, middle, moved)
    ]
    later = [
        dot(w, carry[first_head + i], NT) if c == 1 else None for (i, c), w in zip(units, weights)
    ]
    for (i, c), t, w, weight, x, extra in zip(units, tall, wide, weights, moved, later):
        direct = x[:, DK:]
        if c == 1:
            direct = direct + extra[:, DK:]
            weight = extra[:, :DK].astype(BF16)
        direct_out[t, w] = direct
        coefficient_out[t, w] = weight
    if kept:
        fetch.wait()


def scan_kernel(slots, where, *refs):
    count = len(slots)
    tables, outs, (states, table) = refs[:count], refs[count:-2], refs[-2:]
    for slot, ref in zip(slots, tables):
        table[slot] = ref[...]
    state = jnp.zeros((DK, DK), F32)
    for shard in range(count):
        slot = lax.bitwise_xor(where[0], shard)
        states[slot] = state.astype(BF16)
        if shard < count - 1:
            high = table[slot, 2 * DK : 2 * DK + 1, :].astype(F32)
            low = table[slot, 2 * DK + 8 : 2 * DK + 9, :].astype(F32)
            state = (
                state * (high + low)
                - dot(state.astype(BF16), table[slot, 0:DK, :], NN)
                + table[slot, DK : 2 * DK, :].astype(F32)
            )
    for pair, out in enumerate(outs):
        out[...] = states[2 * pair : 2 * pair + 2]


def fetch_kernel(source, out, arrived):
    copy = pltpu.make_async_copy(source.at[:, 0 : out.shape[1]], out, arrived)
    copy.start()
    copy.wait()


def gather_kernel(*refs):
    *pairs, out = refs
    for i, pair in enumerate(pairs):
        out[i] = pair[1]


def tail_kernel(query, key, value, out):
    out[0] = query[...]
    out[1] = key[...]
    out[2] = value[...]


def project_kernel(heads, owners, where, mine, direct_one, direct_two, weight_one, weight_two, early, matrix, *rest):
    arrived, rest = rest[: heads // 2 + 1], rest[heads // 2 + 1 :]
    *outs, head_out, ordered, states, late, landed = rest
    half_width = early.shape[1]
    copy = pltpu.make_async_copy(matrix.at[:, half_width:], late, landed)
    copy.start()
    for pair in range(heads // 2):
        states[2 * pair] = arrived[pair][0]
        states[2 * pair + 1] = arrived[-1][pair]
    parts = len(owners)
    share = head_out.shape[0] // parts

    @pl.when(pl.program_id(0) == 0)
    def _():
        for head in range(heads):
            at = slice(head * DK, (head + 1) * DK)
            half, inner = divmod(head, heads // 2)
            near = slice(inner * DK, (inner + 1) * DK)
            slot = lax.bitwise_xor(where[0], head)
            total = (direct_one, direct_two)[half][:, near] + dot(
                (weight_one, weight_two)[half][:, near], states[slot], NT
            )
            head_out[:, at] = total.astype(BF16)
        for distance in range(parts):
            owner = owners[distance](mine[0])
            ordered[distance * share : (distance + 1) * share, :] = head_out[
                pl.ds(pl.multiple_of(owner * share, share), share), :
            ]

    for side in range(2):
        if side == 1:
            copy.wait()
        total = dot(ordered[...], (early, late)[side][...], NN)
        at = slice(side * half_width, side * half_width + total.shape[1])
        for distance in range(parts):
            outs[distance][:, at] = total[distance * share : (distance + 1) * share, :].astype(
                outs[distance].dtype
            )


def spec(shape, index):
    return pl.BlockSpec(shape, index)


def call(kernel, grid, in_specs, out_specs, out_shape, scratch, cost, limit, scalars, *args):
    return pl.pallas_call(
        kernel,
        grid_spec=pltpu.PrefetchScalarGridSpec(
            num_scalar_prefetch=scalars,
            grid=grid,
            in_specs=in_specs,
            out_specs=out_specs,
            scratch_shapes=scratch,
        ),
        out_shape=out_shape,
        compiler_params=pltpu.CompilerParams(
            dimension_semantics=("arbitrary",) * len(grid), vmem_limit_bytes=limit << 20
        ),
        cost_estimate=pl.CostEstimate(flops=cost[0], bytes_accessed=cost[1], transcendentals=0),
    )(*args)


def shards(query, key_in, value, gates, beta, conv_query, conv_key, conv_value, out_weight):
    length, width = query.shape
    groups = beta.shape[1]
    taps = conv_query.shape[0]
    ranks = lax.axis_size("seq")
    me = lax.axis_index("seq").astype(jnp.int32)
    spread = groups == ranks
    order = me if spread else jnp.zeros((), jnp.int32)
    shape = jax.ShapeDtypeStruct
    kept = pltpu.VMEM
    here = pl.BlockSpec(memory_space=pltpu.VMEM)
    anywhere = pl.BlockSpec(memory_space=pl.ANY)
    query, key_in, value, gates, beta_rows, conv_query, conv_key, conv_value, out_weight = (
        pltpu.with_memory_space_constraint(data, pltpu.HBM)
        for data in (
            query, key_in, value, gates, beta.T, conv_query, conv_key, conv_value, out_weight
        )
    )
    tail_spec = spec((HALO, width), lambda p: (length // HALO - 1, 0))
    rims = call(
        tail_kernel, (1,), [tail_spec] * 3,
        spec((3, HALO, width), lambda p: (0, 0, 0)), shape((3, HALO, width), BF16),
        [], (0, 3 * HALO * width * 4), LIMIT, 0, query, key_in, value,
    )
    rims = lax.ppermute(rims, "seq", [(i, i + 1) for i in range(ranks - 1)])

    def chunk_specs(c):
        return [spec((CHUNK, width), lambda p, *_: (c, 0))] * 3 + [
            spec((groups, CHUNK), lambda p, *_: (0, c))
        ]

    tap_spec = spec((taps, width), lambda p, *_: (0, 0))
    rim_spec = spec((HALO, width), lambda p, *_: (CHUNK // HALO - 1, 0))
    solved_shape = kept((groups, CHUNK, 2 * DK), F32)
    forward_shape = kept((CHUNK, width), BF16 if PASS_SCORES == 1 else F32)
    conv_scratch = pltpu.VMEM((2, 8 + CHUNK, width), F32)
    cost = (groups * 100_000_000, 4 << 20)

    later_summary, later_decay, later_solved, later_forward = call(
        later_kernel,
        (1,),
        chunk_specs(1) + [rim_spec, rim_spec, tap_spec, tap_spec],
        [here] * 4,
        [kept((groups, 2 * DK, DK), F32), kept((groups, 8, DK), F32), solved_shape, forward_shape],
        [conv_scratch],
        cost,
        LIMIT,
        0,
        key_in, value, gates, beta_rows, key_in, value, conv_key, conv_value,
    )
    packed = 2 * DK + 16
    carry, first_solved, first_forward, *send = call(
        first_kernel,
        (1,),
        chunk_specs(0) + [here, tap_spec, tap_spec, here, here],
        [here] * (3 + groups),
        [kept((groups, 2 * DK, DK), BF16), solved_shape, forward_shape]
        + [kept((packed, DK), BF16)] * groups,
        [pltpu.VMEM((groups, packed, DK), BF16), conv_scratch],
        cost,
        LIMIT,
        1,
        order[None], key_in, value, gates, beta_rows, rims, conv_key, conv_value,
        later_summary, later_decay,
    )

    hops = sorted(range(1, ranks), key=lambda m: (-(m // 2).bit_count(), m))

    def exchange(blocks):
        sent = [lax.ppermute(blocks[m], "seq", [(i, i ^ m) for i in range(ranks)]) for m in hops]
        return [blocks[0]] + sent

    def outputs(half, later_solved, fetch):
        half_spec = spec((length, width // 2), lambda p: (0, half))
        extra_shape = [kept(out_weight.shape, BF16)] if fetch else []
        return call(
            functools.partial(output_kernel, half * groups // 2),
            (1,),
            [half_spec, half_spec, here, spec((taps, width // 2), lambda p: (0, half))]
            + [here] * 5
            + [pl.BlockSpec(memory_space=pl.ANY)],
            [here] * (3 if fetch else 2),
            [kept((length, width // 2), F32), kept((length, width // 2), BF16)] + extra_shape,
            ([pltpu.SemaphoreType.DMA] if fetch else [])
            + [pltpu.VMEM((8 + length, width // 2), F32)],
            (groups * 50_000_000, 2 << 20),
            LIMIT,
            0,
            query, gates, rims, conv_query,
            first_solved, later_solved, first_forward, later_forward, carry, out_weight,
        )

    direct_one, weight_one = outputs(0, later_solved, False)
    if spread:
        arrived = exchange(send)
        arrived, direct_one, weight_one = lax.optimization_barrier((arrived, direct_one, weight_one))
        states = call(
            functools.partial(scan_kernel, [0] + hops),
            (1,),
            [here] * ranks,
            [here] * (ranks // 2),
            [shape((2, DK, DK), BF16)] * (ranks // 2),
            [pltpu.VMEM((ranks, DK, DK), BF16), pltpu.VMEM((ranks, packed, DK), BF16)],
            (ranks * 4_000_000, 1 << 20),
            LIMIT,
            1,
            me[None], *arrived,
        )
        states, later_solved = lax.optimization_barrier((states, later_solved))
        direct_two, weight_two = outputs(1, later_solved, False)
        states = [states[0]] + [
            lax.ppermute(states[d], "seq", [(i, i ^ (2 * d)) for i in range(ranks)])
            for d in range(1, ranks // 2)
        ]
        states, direct_two, weight_two = lax.optimization_barrier((states, direct_two, weight_two))
        aside = call(
            gather_kernel, (1,), [here] * (ranks // 2), here,
            shape((ranks // 2, DK, DK), BF16), [], (0, 1 << 18), LIMIT, 0, *states,
        )
        aside, source = lax.optimization_barrier((aside, out_weight))
        states = states + [lax.ppermute(aside, "seq", [(i, i ^ 1) for i in range(ranks)])]
    else:
        direct_two, weight_two = outputs(1, later_solved, False)
        every = lax.all_gather(jnp.stack(send), "seq")
        product, offset = every[:, :, :DK].astype(F32), every[:, :, DK : 2 * DK].astype(F32)
        decay = every[:, :, 2 * DK : 2 * DK + 1].astype(F32) + every[:, :, 2 * DK + 8 : 2 * DK + 9].astype(F32)
        state = jnp.zeros((groups, DK, DK), F32)
        states = state
        for shard in range(ranks):
            states = jnp.where(me == shard, state, states)
            moved = jnp.einsum("hij,hjk->hik", state, product[shard], precision=lax.Precision.HIGHEST)
            state = state * decay[shard] - moved + offset[shard]
        states = states.astype(BF16)
        source = out_weight
        states = [states[i : i + 2] for i in range(0, groups, 2)] + [states[1::2]]

    parts = lax.axis_size("head")
    mine = lax.axis_index("head").astype(jnp.int32)
    share = length // parts
    model = out_weight.shape[1]
    if parts == 4:
        owners = (
            lambda z: z,
            lambda z: jnp.where(lax.rem(z, 2) == 0, 3, 0),
            lambda z: jnp.where(z < 2, 2, 1),
            lambda z: lax.rem(2 * z + 1, 5),
        )
    else:
        owners = [lambda z, d=d: lax.rem(z + d, parts) for d in range(parts)]
    half = model // 2
    early = call(
        fetch_kernel, (1,), [anywhere], here, kept((width, half), BF16),
        [pltpu.SemaphoreType.DMA], (0, width * model * 2), LIMIT, 0, source,
    )
    own, *leaving = call(
        functools.partial(project_kernel, groups, owners),
        (1,),
        [here] * 5 + [anywhere] + [here] * (groups // 2 + 1),
        [here] * parts,
        [kept((share, model), F32)] + [kept((share, model), BF16)] * (parts - 1),
        [pltpu.VMEM((length, width), BF16)] * 2
        + [
            pltpu.VMEM((groups, DK, DK), BF16),
            pltpu.VMEM((width, model - half), BF16),
            pltpu.SemaphoreType.DMA,
        ],
        (2 * length * width * model, width * model * 2),
        LIMIT,
        2,
        order[None], mine[None], direct_one, direct_two, weight_one, weight_two, early, source, *states,
    )
    if parts == 4:
        near, inward, last = leaving
        middle = (mine == 1) | (mine == 2)
        near = lax.ppermute(near, "head", [(0, 1), (1, 0), (2, 3), (3, 2)]).astype(F32)
        crossed = lax.ppermute(inward, "head", [(1, 2), (2, 1)])
        skipped = lax.ppermute(inward, "head", [(0, 2), (3, 1)])
        joined = (last.astype(F32) + jnp.where(middle, near, 0.0)).astype(BF16)
        joined = lax.ppermute(joined, "head", [(0, 1), (3, 2), (1, 3), (2, 0)])
        arrived = [jnp.where(middle, 0.0, near), crossed, skipped, joined]
    else:
        arrived = [
            lax.ppermute(part, "head", [(i, (i + d) % parts) for i in range(parts)])
            for d, part in enumerate(leaving, 1)
        ]
    total = own
    for part in arrived:
        total = total + part.astype(F32)
    return total.astype(BF16)


def solution(mesh):
    in_specs = (
        P("seq", "head"),
        P("seq", "head"),
        P("seq", "head"),
        P("seq", "head"),
        P("seq", "head"),
        P(None, "head"),
        P(None, "head"),
        P(None, "head"),
        P("head", None),
    )
    out_specs = P(("seq", "head"), None)
    return jax.shard_map(shards, mesh=mesh, in_specs=in_specs, out_specs=out_specs, check_vma=False)
```

```python
import functools

import jax
import jax.numpy as jnp
from jax import lax
from jax.experimental import pallas as pl
from jax.experimental.pallas import tpu as pltpu
from jax.sharding import PartitionSpec as P

DK = 128
CHUNK = 128
MID = 63
HALO = 16
BASE = 16
LIMIT = 32
F32 = jnp.float32
BF16 = jnp.bfloat16

PASS_A = 3
PASS_SOLVE = 3
PASS_UW = 3
PASS_PO = 3
PASS_COMP = 2
PASS_SCORES = 1
PASS_SU = 3

NN = (((1,), (0,)), ((), ()))
NT = (((1,), (1,)), ((), ()))
TN = (((0,), (0,)), ((), ()))


def dot(left, right, dims):
    return lax.dot_general(left, right, dims, preferred_element_type=F32)


def split(data):
    high = data.astype(BF16)
    return high, (data - high.astype(F32)).astype(BF16)


def mm(left, right, dims, passes):
    if passes == 1:
        return dot(left.astype(BF16), right.astype(BF16), dims)
    left_high, left_low = split(left)
    if passes == 2:
        right = right.astype(BF16)
        return dot(left_high, right, dims) + dot(left_low, right, dims)
    right_high, right_low = split(right)
    return dot(left_high, right_high, dims) + (
        dot(left_low, right_high, dims) + dot(left_high, right_low, dims)
    )


def conv_silu(scratch, data, before, taps):
    count, width = data.shape
    scratch[0:8, :] = before.astype(F32)
    scratch[8 : 8 + count, :] = data.astype(F32)
    number = taps.shape[0]
    total = taps[number - 1 : number, :].astype(F32) * scratch[8 : 8 + count, :]
    for tap in range(number - 1):
        first = 8 - (number - 1) + tap
        total = total + taps[tap : tap + 1, :].astype(F32) * scratch[first : first + count, :]
    return total * lax.logistic(total)


def normalize(data):
    return data * lax.rsqrt(jnp.sum(data * data, axis=-1, keepdims=True) + 1e-06)


def iotas():
    rows = lax.broadcasted_iota(jnp.int32, (CHUNK, CHUNK), 0)
    columns = lax.broadcasted_iota(jnp.int32, (CHUNK, CHUNK), 1)
    return rows, columns


def cumulate(gates, rows, columns):
    ones = jnp.where(columns <= rows, 1.0, 0.0).astype(BF16)
    return dot(ones, gates, NN)


def inverse_blocks(matrices, rows, columns):
    lanes = lax.broadcasted_iota(jnp.int32, (8, CHUNK), 1)
    inner = lax.broadcasted_iota(jnp.int32, (8, CHUNK), 0)
    tiles = BASE // 8
    packed, solved = [], []
    for matrix in matrices:
        pack = []
        for t in range(tiles):
            total = jnp.zeros((8, CHUNK), F32)
            for b in range(CHUNK // BASE):
                first = b * BASE + t * 8
                total = jnp.where(lanes // BASE == b, matrix[first : first + 8, :], total)
            pack.append(total)
        packed.append(pack)
        solved.append([jnp.where(lanes % BASE == inner + 8 * t, 1.0, 0.0) for t in range(tiles)])
    for j in range(BASE - 1):
        pick = (lanes // BASE) * BASE + j
        for pack, block in zip(packed, solved):
            row = jnp.broadcast_to(block[j // 8][j % 8 : j % 8 + 1, :], (8, CHUNK))
            for t in range(j // 8, tiles):
                factor = jnp.take_along_axis(pack[t], pick, axis=1)
                block[t] = block[t] - factor * row
    results = []
    for block in solved:
        tall = jnp.concatenate(block * (CHUNK // BASE), axis=0)
        results.append(jnp.where(rows // BASE == columns // BASE, tall, 0.0))
    size = BASE
    while size < CHUNK:
        here = (rows // (2 * size) == columns // (2 * size)) & (rows // size != columns // size)
        moved = [
            mm(jnp.where(here, matrix, 0.0), result, NN, PASS_SOLVE)
            for matrix, result in zip(matrices, results)
        ]
        results = [
            result - mm(result, move, NN, PASS_SOLVE) for result, move in zip(results, moved)
        ]
        size *= 2
    return results


def column_of(row, rows, columns):
    return jnp.sum(jnp.where(rows == columns, row, 0.0), axis=-1, keepdims=True)


def chunk_terms(keys, values, gates, betas, rows, columns):
    cumul = [cumulate(g, rows, columns) for g in gates]
    middle = [c[MID : MID + 1, :] for c in cumul]
    final = [c[CHUNK - 1 : CHUNK, :] for c in cumul]
    forward = [k * jnp.exp(m - c) for k, m, c in zip(keys, middle, cumul)]
    backward = [k * jnp.exp(c - m) for k, m, c in zip(keys, middle, cumul)]
    coupling = [mm(b, f, NT, PASS_A) for b, f in zip(backward, forward)]
    strict = [jnp.where(columns < rows, a * b, 0.0) for a, b in zip(coupling, betas)]
    solver = inverse_blocks(strict, rows, columns)
    sides = [
        jnp.concatenate([beta * b * jnp.exp(m), beta * v], axis=-1)
        for beta, b, m, v in zip(betas, backward, middle, values)
    ]
    solved = [mm(x, side, NN, PASS_UW) for x, side in zip(solver, sides)]
    trailing = [f * jnp.exp(e - m) for f, e, m in zip(forward, final, middle)]
    summary = [mm(u, t, TN, PASS_PO) for u, t in zip(solved, trailing)]
    return [jnp.exp(e) for e in final], summary, solved, forward


def chunk_of(key, value, gate, beta, key_rim, value_rim, key_taps, value_taps, scratch):
    rows, columns = iotas()
    keys_all = conv_silu(scratch.at[0], key[...], key_rim[8:16, :], key_taps)
    values_all = conv_silu(scratch.at[1], value[...], value_rim[8:16, :], value_taps)
    heads = range(beta.shape[0])
    parts = [slice(i * DK, (i + 1) * DK) for i in heads]
    terms = chunk_terms(
        [normalize(keys_all[:, at]) for at in parts],
        [values_all[:, at] for at in parts],
        [gate[:, at] for at in parts],
        [column_of(beta[i : i + 1, :], rows, columns) for i in heads],
        rows,
        columns,
    )
    return heads, parts, rows, columns, terms


def later_kernel(
    key, value, gate, beta, key_rim, value_rim, key_taps, value_taps,
    summary_out, decay_out, solved_out, forward_out, scratch,
):
    _, parts, _, _, terms = chunk_of(
        key, value, gate, beta, key_rim, value_rim, key_taps, value_taps, scratch
    )
    for i, (at, decay, summary, solved, forward) in enumerate(zip(parts, *terms)):
        summary_out[i] = summary
        decay_out[i] = jnp.broadcast_to(decay, (8, DK))
        solved_out[i] = solved
        forward_out[:, at] = forward.astype(forward_out.dtype)


def first_kernel(
    where, key, value, gate, beta, rims, key_taps, value_taps, later_summary, later_decay,
    carry_out, solved_out, forward_out, *rest,
):
    *send_outs, send, scratch = rest
    heads, parts, rows, columns, terms = chunk_of(
        key, value, gate, beta, rims.at[1], rims.at[2], key_taps, value_taps, scratch
    )
    carries, moves = [], []
    for i, (at, decay, summary, solved, forward) in enumerate(zip(parts, *terms)):
        solved_out[i] = solved
        forward_out[:, at] = forward.astype(forward_out.dtype)
        steady = jnp.where(rows == columns, decay, 0.0)
        carry = jnp.concatenate([steady - summary[:DK], summary[DK:]], axis=0)
        carry_out[i] = carry.astype(BF16)
        carries.append(carry)
    for i, carry in enumerate(carries):
        moves.append(mm(carry, later_summary[i, :DK, :], NN, PASS_COMP))
    for head, decay, summary, moved in zip(heads, terms[0], terms[1], moves):
        after = later_decay[head, 0:1, :]
        product = summary[:DK] * after + moved[:DK]
        offset = summary[DK:] * after - moved[DK:] + later_summary[head, DK:, :]
        both = decay * after
        high = both.astype(BF16)
        low = (both - high.astype(F32)).astype(BF16)
        slot = lax.bitwise_xor(head, where[0])
        send[slot, 0:DK, :] = product.astype(BF16)
        send[slot, DK : 2 * DK, :] = offset.astype(BF16)
        send[slot, 2 * DK : 2 * DK + 16, :] = jnp.concatenate(
            [jnp.broadcast_to(high, (8, DK)), jnp.broadcast_to(low, (8, DK))], axis=0
        )
    for slot, out in enumerate(send_outs):
        out[...] = send[slot]


def output_kernel(
    first_head, query, gate, rims, query_taps,
    first_solved, later_solved, first_forward, later_forward, carry, matrix,
    direct_out, coefficient_out, *rest,
):
    *kept, scratch = rest
    if kept:
        matrix_out, arrived = kept
        fetch = pltpu.make_async_copy(matrix, matrix_out, arrived)
        fetch.start()
    step_heads = query.shape[1] // DK
    query_rim = rims[0, :, first_head * DK : first_head * DK + query.shape[1]]
    rows, columns = iotas()
    queries_all = conv_silu(scratch, query[...], query_rim[8:16, :], query_taps)
    units = [(i, c) for i in range(step_heads) for c in range(2)]
    wide = [slice(i * DK, (i + 1) * DK) for i, _ in units]
    tall = [slice(c * CHUNK, (c + 1) * CHUNK) for _, c in units]
    solved = [(first_solved, later_solved)[c][first_head + i] for i, c in units]
    forward = [
        (first_forward, later_forward)[c][:, (first_head + i) * DK : (first_head + i + 1) * DK]
        for i, c in units
    ]
    cumul = [cumulate(gate[t, w], rows, columns) for t, w in zip(tall, wide)]
    middle = [c[MID : MID + 1, :] for c in cumul]
    queries = [normalize(queries_all[t, w]) * DK ** (-0.5) for t, w in zip(tall, wide)]
    queried = [q * jnp.exp(c - m) for q, c, m in zip(queries, cumul, middle)]
    scores = [mm(q, f, NT, PASS_SCORES) for q, f in zip(queried, forward)]
    scores = [jnp.where(columns <= rows, x, 0.0) for x in scores]
    moved = [mm(x, u, NN, PASS_SU) for x, u in zip(scores, solved)]
    weights = [
        (q * jnp.exp(m) - x[:, :DK]).astype(BF16) for q, m, x in zip(queried, middle, moved)
    ]
    later = [
        dot(w, carry[first_head + i], NT) if c == 1 else None for (i, c), w in zip(units, weights)
    ]
    for (i, c), t, w, weight, x, extra in zip(units, tall, wide, weights, moved, later):
        direct = x[:, DK:]
        if c == 1:
            direct = direct + extra[:, DK:]
            weight = extra[:, :DK].astype(BF16)
        direct_out[t, w] = direct
        coefficient_out[t, w] = weight
    if kept:
        fetch.wait()


def scan_kernel(slots, where, *refs):
    count = len(slots)
    tables, outs, (states, table) = refs[:count], refs[count:-2], refs[-2:]
    for slot, ref in zip(slots, tables):
        table[slot] = ref[...]
    state = jnp.zeros((DK, DK), F32)
    for shard in range(count):
        slot = lax.bitwise_xor(where[0], shard)
        states[slot] = state.astype(BF16)
        if shard < count - 1:
            high = table[slot, 2 * DK : 2 * DK + 1, :].astype(F32)
            low = table[slot, 2 * DK + 8 : 2 * DK + 9, :].astype(F32)
            state = (
                state * (high + low)
                - dot(state.astype(BF16), table[slot, 0:DK, :], NN)
                + table[slot, DK : 2 * DK, :].astype(F32)
            )
    for pair, out in enumerate(outs):
        out[...] = states[2 * pair : 2 * pair + 2]


def fetch_kernel(source, out, arrived):
    copy = pltpu.make_async_copy(source.at[:, 0 : out.shape[1]], out, arrived)
    copy.start()
    copy.wait()


def gather_kernel(*refs):
    *pairs, out = refs
    for i, pair in enumerate(pairs):
        out[i] = pair[1]


def tail_kernel(query, key, value, out):
    out[0] = query[...]
    out[1] = key[...]
    out[2] = value[...]


def project_kernel(heads, owners, where, mine, direct_one, direct_two, weight_one, weight_two, early, matrix, *rest):
    arrived, rest = rest[: heads // 2 + 1], rest[heads // 2 + 1 :]
    *outs, head_out, ordered, states, late, landed = rest
    half_width = early.shape[1]
    copy = pltpu.make_async_copy(matrix.at[:, half_width:], late, landed)
    copy.start()
    for pair in range(heads // 2):
        states[2 * pair] = arrived[pair][0]
        states[2 * pair + 1] = arrived[-1][pair]
    parts = len(owners)
    share = head_out.shape[0] // parts

    @pl.when(pl.program_id(0) == 0)
    def _():
        for head in range(heads):
            at = slice(head * DK, (head + 1) * DK)
            half, inner = divmod(head, heads // 2)
            near = slice(inner * DK, (inner + 1) * DK)
            slot = lax.bitwise_xor(where[0], head)
            total = (direct_one, direct_two)[half][:, near] + dot(
                (weight_one, weight_two)[half][:, near], states[slot], NT
            )
            head_out[:, at] = total.astype(BF16)
        for distance in range(parts):
            owner = owners[distance](mine[0])
            ordered[distance * share : (distance + 1) * share, :] = head_out[
                pl.ds(pl.multiple_of(owner * share, share), share), :
            ]

    for side in range(2):
        if side == 1:
            copy.wait()
        total = dot(ordered[...], (early, late)[side][...], NN)
        at = slice(side * half_width, side * half_width + total.shape[1])
        for distance in range(parts):
            outs[distance][:, at] = total[distance * share : (distance + 1) * share, :].astype(
                outs[distance].dtype
            )


def spec(shape, index):
    return pl.BlockSpec(shape, index)


def call(kernel, grid, in_specs, out_specs, out_shape, scratch, cost, limit, scalars, *args):
    return pl.pallas_call(
        kernel,
        grid_spec=pltpu.PrefetchScalarGridSpec(
            num_scalar_prefetch=scalars,
            grid=grid,
            in_specs=in_specs,
            out_specs=out_specs,
            scratch_shapes=scratch,
        ),
        out_shape=out_shape,
        compiler_params=pltpu.CompilerParams(
            dimension_semantics=("arbitrary",) * len(grid), vmem_limit_bytes=limit << 20
        ),
        cost_estimate=pl.CostEstimate(flops=cost[0], bytes_accessed=cost[1], transcendentals=0),
    )(*args)


def shards(query, key_in, value, gates, beta, conv_query, conv_key, conv_value, out_weight):
    length, width = query.shape
    groups = beta.shape[1]
    taps = conv_query.shape[0]
    ranks = lax.axis_size("seq")
    me = lax.axis_index("seq").astype(jnp.int32)
    spread = groups == ranks
    order = me if spread else jnp.zeros((), jnp.int32)
    shape = jax.ShapeDtypeStruct
    kept = pltpu.VMEM
    here = pl.BlockSpec(memory_space=pltpu.VMEM)
    anywhere = pl.BlockSpec(memory_space=pl.ANY)
    query, key_in, value, gates, beta_rows, conv_query, conv_key, conv_value, out_weight = (
        pltpu.with_memory_space_constraint(data, pltpu.HBM)
        for data in (
            query, key_in, value, gates, beta.T, conv_query, conv_key, conv_value, out_weight
        )
    )
    tail_spec = spec((HALO, width), lambda p: (length // HALO - 1, 0))
    rims = call(
        tail_kernel, (1,), [tail_spec] * 3,
        spec((3, HALO, width), lambda p: (0, 0, 0)), shape((3, HALO, width), BF16),
        [], (0, 3 * HALO * width * 4), LIMIT, 0, query, key_in, value,
    )
    rims = lax.ppermute(rims, "seq", [(i, i + 1) for i in range(ranks - 1)])

    def chunk_specs(c):
        return [spec((CHUNK, width), lambda p, *_: (c, 0))] * 3 + [
            spec((groups, CHUNK), lambda p, *_: (0, c))
        ]

    tap_spec = spec((taps, width), lambda p, *_: (0, 0))
    rim_spec = spec((HALO, width), lambda p, *_: (CHUNK // HALO - 1, 0))
    solved_shape = kept((groups, CHUNK, 2 * DK), F32)
    forward_shape = kept((CHUNK, width), BF16 if PASS_SCORES == 1 else F32)
    conv_scratch = pltpu.VMEM((2, 8 + CHUNK, width), F32)
    cost = (groups * 100_000_000, 4 << 20)

    later_summary, later_decay, later_solved, later_forward = call(
        later_kernel,
        (1,),
        chunk_specs(1) + [rim_spec, rim_spec, tap_spec, tap_spec],
        [here] * 4,
        [kept((groups, 2 * DK, DK), F32), kept((groups, 8, DK), F32), solved_shape, forward_shape],
        [conv_scratch],
        cost,
        LIMIT,
        0,
        key_in, value, gates, beta_rows, key_in, value, conv_key, conv_value,
    )
    packed = 2 * DK + 16
    carry, first_solved, first_forward, *send = call(
        first_kernel,
        (1,),
        chunk_specs(0) + [here, tap_spec, tap_spec, here, here],
        [here] * (3 + groups),
        [kept((groups, 2 * DK, DK), BF16), solved_shape, forward_shape]
        + [kept((packed, DK), BF16)] * groups,
        [pltpu.VMEM((groups, packed, DK), BF16), conv_scratch],
        cost,
        LIMIT,
        1,
        order[None], key_in, value, gates, beta_rows, rims, conv_key, conv_value,
        later_summary, later_decay,
    )

    hops = sorted(range(1, ranks), key=lambda m: (-(m // 2).bit_count(), m))

    def exchange(blocks):
        sent = [lax.ppermute(blocks[m], "seq", [(i, i ^ m) for i in range(ranks)]) for m in hops]
        return [blocks[0]] + sent

    def outputs(half, later_solved, fetch):
        half_spec = spec((length, width // 2), lambda p: (0, half))
        extra_shape = [kept(out_weight.shape, BF16)] if fetch else []
        return call(
            functools.partial(output_kernel, half * groups // 2),
            (1,),
            [half_spec, half_spec, here, spec((taps, width // 2), lambda p: (0, half))]
            + [here] * 5
            + [pl.BlockSpec(memory_space=pl.ANY)],
            [here] * (3 if fetch else 2),
            [kept((length, width // 2), F32), kept((length, width // 2), BF16)] + extra_shape,
            ([pltpu.SemaphoreType.DMA] if fetch else [])
            + [pltpu.VMEM((8 + length, width // 2), F32)],
            (groups * 50_000_000, 2 << 20),
            LIMIT,
            0,
            query, gates, rims, conv_query,
            first_solved, later_solved, first_forward, later_forward, carry, out_weight,
        )

    direct_one, weight_one = outputs(0, later_solved, False)
    if spread:
        arrived = exchange(send)
        arrived, direct_one, weight_one = lax.optimization_barrier((arrived, direct_one, weight_one))
        states = call(
            functools.partial(scan_kernel, [0] + hops),
            (1,),
            [here] * ranks,
            [here] * (ranks // 2),
            [shape((2, DK, DK), BF16)] * (ranks // 2),
            [pltpu.VMEM((ranks, DK, DK), BF16), pltpu.VMEM((ranks, packed, DK), BF16)],
            (ranks * 4_000_000, 1 << 20),
            LIMIT,
            1,
            me[None], *arrived,
        )
        states, later_solved = lax.optimization_barrier((states, later_solved))
        direct_two, weight_two = outputs(1, later_solved, False)
        states = [states[0]] + [
            lax.ppermute(states[d], "seq", [(i, i ^ (2 * d)) for i in range(ranks)])
            for d in range(1, ranks // 2)
        ]
        states, direct_two, weight_two = lax.optimization_barrier((states, direct_two, weight_two))
        aside = call(
            gather_kernel, (1,), [here] * (ranks // 2), here,
            shape((ranks // 2, DK, DK), BF16), [], (0, 1 << 18), LIMIT, 0, *states,
        )
        aside, source = lax.optimization_barrier((aside, out_weight))
        states = states + [lax.ppermute(aside, "seq", [(i, i ^ 1) for i in range(ranks)])]
    else:
        direct_two, weight_two = outputs(1, later_solved, False)
        every = lax.all_gather(jnp.stack(send), "seq")
        product, offset = every[:, :, :DK].astype(F32), every[:, :, DK : 2 * DK].astype(F32)
        decay = every[:, :, 2 * DK : 2 * DK + 1].astype(F32) + every[:, :, 2 * DK + 8 : 2 * DK + 9].astype(F32)
        state = jnp.zeros((groups, DK, DK), F32)
        states = state
        for shard in range(ranks):
            states = jnp.where(me == shard, state, states)
            moved = jnp.einsum("hij,hjk->hik", state, product[shard], precision=lax.Precision.HIGHEST)
            state = state * decay[shard] - moved + offset[shard]
        states = states.astype(BF16)
        source = out_weight
        states = [states[i : i + 2] for i in range(0, groups, 2)] + [states[1::2]]

    parts = lax.axis_size("head")
    mine = lax.axis_index("head").astype(jnp.int32)
    share = length // parts
    model = out_weight.shape[1]
    if parts == 4:
        owners = (
            lambda z: z,
            lambda z: jnp.where(lax.rem(z, 2) == 0, 3, 0),
            lambda z: jnp.where(z < 2, 2, 1),
            lambda z: lax.rem(2 * z + 1, 5),
        )
    else:
        owners = [lambda z, d=d: lax.rem(z + d, parts) for d in range(parts)]
    half = 2 * (model // 3)
    early = call(
        fetch_kernel, (1,), [anywhere], here, kept((width, half), BF16),
        [pltpu.SemaphoreType.DMA], (0, width * model * 2), LIMIT, 0, source,
    )
    own, *leaving = call(
        functools.partial(project_kernel, groups, owners),
        (1,),
        [here] * 5 + [anywhere] + [here] * (groups // 2 + 1),
        [here] * parts,
        [kept((share, model), F32)] + [kept((share, model), BF16)] * (parts - 1),
        [pltpu.VMEM((length, width), BF16)] * 2
        + [
            pltpu.VMEM((groups, DK, DK), BF16),
            pltpu.VMEM((width, model - half), BF16),
            pltpu.SemaphoreType.DMA,
        ],
        (2 * length * width * model, width * model * 2),
        LIMIT,
        2,
        order[None], mine[None], direct_one, direct_two, weight_one, weight_two, early, source, *states,
    )
    if parts == 4:
        near, inward, last = leaving
        middle = (mine == 1) | (mine == 2)
        near = lax.ppermute(near, "head", [(0, 1), (1, 0), (2, 3), (3, 2)]).astype(F32)
        crossed = lax.ppermute(inward, "head", [(1, 2), (2, 1)])
        skipped = lax.ppermute(inward, "head", [(0, 2), (3, 1)])
        joined = (last.astype(F32) + jnp.where(middle, near, 0.0)).astype(BF16)
        joined = lax.ppermute(joined, "head", [(0, 1), (3, 2), (1, 3), (2, 0)])
        arrived = [jnp.where(middle, 0.0, near), crossed, skipped, joined]
    else:
        arrived = [
            lax.ppermute(part, "head", [(i, (i + d) % parts) for i in range(parts)])
            for d, part in enumerate(leaving, 1)
        ]
    total = own
    for part in arrived:
        total = total + part.astype(F32)
    return total.astype(BF16)


def solution(mesh):
    in_specs = (
        P("seq", "head"),
        P("seq", "head"),
        P("seq", "head"),
        P("seq", "head"),
        P("seq", "head"),
        P(None, "head"),
        P(None, "head"),
        P(None, "head"),
        P("head", None),
    )
    out_specs = P(("seq", "head"), None)
    return jax.shard_map(shards, mesh=mesh, in_specs=in_specs, out_specs=out_specs, check_vma=False)
```

```python
import functools

import jax
import jax.numpy as jnp
from jax import lax
from jax.experimental import pallas as pl
from jax.experimental.pallas import tpu as pltpu
from jax.sharding import PartitionSpec as P

DK = 128
CHUNK = 128
MID = 63
HALO = 16
BASE = 16
LIMIT = 32
F32 = jnp.float32
BF16 = jnp.bfloat16

PASS_A = 3
PASS_SOLVE = 3
PASS_UW = 3
PASS_PO = 3
PASS_COMP = 2
PASS_SCORES = 1
PASS_SU = 3

NN = (((1,), (0,)), ((), ()))
NT = (((1,), (1,)), ((), ()))
TN = (((0,), (0,)), ((), ()))


def dot(left, right, dims):
    return lax.dot_general(left, right, dims, preferred_element_type=F32)


def split(data):
    high = data.astype(BF16)
    return high, (data - high.astype(F32)).astype(BF16)


def mm(left, right, dims, passes):
    if passes == 1:
        return dot(left.astype(BF16), right.astype(BF16), dims)
    left_high, left_low = split(left)
    if passes == 2:
        right = right.astype(BF16)
        return dot(left_high, right, dims) + dot(left_low, right, dims)
    right_high, right_low = split(right)
    return dot(left_high, right_high, dims) + (
        dot(left_low, right_high, dims) + dot(left_high, right_low, dims)
    )


def conv_silu(scratch, data, before, taps):
    count, width = data.shape
    scratch[0:8, :] = before.astype(F32)
    scratch[8 : 8 + count, :] = data.astype(F32)
    number = taps.shape[0]
    total = taps[number - 1 : number, :].astype(F32) * scratch[8 : 8 + count, :]
    for tap in range(number - 1):
        first = 8 - (number - 1) + tap
        total = total + taps[tap : tap + 1, :].astype(F32) * scratch[first : first + count, :]
    return total * lax.logistic(total)


def normalize(data):
    return data * lax.rsqrt(jnp.sum(data * data, axis=-1, keepdims=True) + 1e-06)


def iotas():
    rows = lax.broadcasted_iota(jnp.int32, (CHUNK, CHUNK), 0)
    columns = lax.broadcasted_iota(jnp.int32, (CHUNK, CHUNK), 1)
    return rows, columns


def cumulate(gates, rows, columns):
    ones = jnp.where(columns <= rows, 1.0, 0.0).astype(BF16)
    return dot(ones, gates, NN)


def inverse_blocks(matrices, rows, columns):
    lanes = lax.broadcasted_iota(jnp.int32, (8, CHUNK), 1)
    inner = lax.broadcasted_iota(jnp.int32, (8, CHUNK), 0)
    tiles = BASE // 8
    packed, solved = [], []
    for matrix in matrices:
        pack = []
        for t in range(tiles):
            total = jnp.zeros((8, CHUNK), F32)
            for b in range(CHUNK // BASE):
                first = b * BASE + t * 8
                total = jnp.where(lanes // BASE == b, matrix[first : first + 8, :], total)
            pack.append(total)
        packed.append(pack)
        solved.append([jnp.where(lanes % BASE == inner + 8 * t, 1.0, 0.0) for t in range(tiles)])
    for j in range(BASE - 1):
        pick = (lanes // BASE) * BASE + j
        for pack, block in zip(packed, solved):
            row = jnp.broadcast_to(block[j // 8][j % 8 : j % 8 + 1, :], (8, CHUNK))
            for t in range(j // 8, tiles):
                factor = jnp.take_along_axis(pack[t], pick, axis=1)
                block[t] = block[t] - factor * row
    results = []
    for block in solved:
        tall = jnp.concatenate(block * (CHUNK // BASE), axis=0)
        results.append(jnp.where(rows // BASE == columns // BASE, tall, 0.0))
    size = BASE
    while size < CHUNK:
        here = (rows // (2 * size) == columns // (2 * size)) & (rows // size != columns // size)
        moved = [
            mm(jnp.where(here, matrix, 0.0), result, NN, PASS_SOLVE)
            for matrix, result in zip(matrices, results)
        ]
        results = [
            result - mm(result, move, NN, PASS_SOLVE) for result, move in zip(results, moved)
        ]
        size *= 2
    return results


def column_of(row, rows, columns):
    return jnp.sum(jnp.where(rows == columns, row, 0.0), axis=-1, keepdims=True)


def chunk_terms(keys, values, gates, betas, rows, columns):
    cumul = [cumulate(g, rows, columns) for g in gates]
    middle = [c[MID : MID + 1, :] for c in cumul]
    final = [c[CHUNK - 1 : CHUNK, :] for c in cumul]
    forward = [k * jnp.exp(m - c) for k, m, c in zip(keys, middle, cumul)]
    backward = [k * jnp.exp(c - m) for k, m, c in zip(keys, middle, cumul)]
    coupling = [mm(b, f, NT, PASS_A) for b, f in zip(backward, forward)]
    strict = [jnp.where(columns < rows, a * b, 0.0) for a, b in zip(coupling, betas)]
    solver = inverse_blocks(strict, rows, columns)
    sides = [
        jnp.concatenate([beta * b * jnp.exp(m), beta * v], axis=-1)
        for beta, b, m, v in zip(betas, backward, middle, values)
    ]
    solved = [mm(x, side, NN, PASS_UW) for x, side in zip(solver, sides)]
    trailing = [f * jnp.exp(e - m) for f, e, m in zip(forward, final, middle)]
    summary = [mm(u, t, TN, PASS_PO) for u, t in zip(solved, trailing)]
    return [jnp.exp(e) for e in final], summary, solved, forward


def chunk_of(key, value, gate, beta, key_rim, value_rim, key_taps, value_taps, scratch):
    rows, columns = iotas()
    keys_all = conv_silu(scratch.at[0], key[...], key_rim[8:16, :], key_taps)
    values_all = conv_silu(scratch.at[1], value[...], value_rim[8:16, :], value_taps)
    heads = range(beta.shape[0])
    parts = [slice(i * DK, (i + 1) * DK) for i in heads]
    terms = chunk_terms(
        [normalize(keys_all[:, at]) for at in parts],
        [values_all[:, at] for at in parts],
        [gate[:, at] for at in parts],
        [column_of(beta[i : i + 1, :], rows, columns) for i in heads],
        rows,
        columns,
    )
    return heads, parts, rows, columns, terms


def later_kernel(
    key, value, gate, beta, key_rim, value_rim, key_taps, value_taps,
    summary_out, decay_out, solved_out, forward_out, scratch,
):
    _, parts, _, _, terms = chunk_of(
        key, value, gate, beta, key_rim, value_rim, key_taps, value_taps, scratch
    )
    for i, (at, decay, summary, solved, forward) in enumerate(zip(parts, *terms)):
        summary_out[i] = summary
        decay_out[i] = jnp.broadcast_to(decay, (8, DK))
        solved_out[i] = solved
        forward_out[:, at] = forward.astype(forward_out.dtype)


def first_kernel(
    where, key, value, gate, beta, rims, key_taps, value_taps, later_summary, later_decay,
    carry_out, solved_out, forward_out, *rest,
):
    *send_outs, send, scratch = rest
    heads, parts, rows, columns, terms = chunk_of(
        key, value, gate, beta, rims.at[1], rims.at[2], key_taps, value_taps, scratch
    )
    carries, moves = [], []
    for i, (at, decay, summary, solved, forward) in enumerate(zip(parts, *terms)):
        solved_out[i] = solved
        forward_out[:, at] = forward.astype(forward_out.dtype)
        steady = jnp.where(rows == columns, decay, 0.0)
        carry = jnp.concatenate([steady - summary[:DK], summary[DK:]], axis=0)
        carry_out[i] = carry.astype(BF16)
        carries.append(carry)
    for i, carry in enumerate(carries):
        moves.append(mm(carry, later_summary[i, :DK, :], NN, PASS_COMP))
    for head, decay, summary, moved in zip(heads, terms[0], terms[1], moves):
        after = later_decay[head, 0:1, :]
        product = summary[:DK] * after + moved[:DK]
        offset = summary[DK:] * after - moved[DK:] + later_summary[head, DK:, :]
        both = decay * after
        high = both.astype(BF16)
        low = (both - high.astype(F32)).astype(BF16)
        slot = lax.bitwise_xor(head, where[0])
        send[slot, 0:DK, :] = product.astype(BF16)
        send[slot, DK : 2 * DK, :] = offset.astype(BF16)
        send[slot, 2 * DK : 2 * DK + 16, :] = jnp.concatenate(
            [jnp.broadcast_to(high, (8, DK)), jnp.broadcast_to(low, (8, DK))], axis=0
        )
    for slot, out in enumerate(send_outs):
        out[...] = send[slot]


def output_kernel(
    first_head, query, gate, rims, query_taps,
    first_solved, later_solved, first_forward, later_forward, carry, matrix,
    direct_out, coefficient_out, *rest,
):
    *kept, scratch = rest
    if kept:
        matrix_out, arrived = kept
        fetch = pltpu.make_async_copy(matrix, matrix_out, arrived)
        fetch.start()
    step_heads = query.shape[1] // DK
    query_rim = rims[0, :, first_head * DK : first_head * DK + query.shape[1]]
    rows, columns = iotas()
    queries_all = conv_silu(scratch, query[...], query_rim[8:16, :], query_taps)
    units = [(i, c) for i in range(step_heads) for c in range(2)]
    wide = [slice(i * DK, (i + 1) * DK) for i, _ in units]
    tall = [slice(c * CHUNK, (c + 1) * CHUNK) for _, c in units]
    solved = [(first_solved, later_solved)[c][first_head + i] for i, c in units]
    forward = [
        (first_forward, later_forward)[c][:, (first_head + i) * DK : (first_head + i + 1) * DK]
        for i, c in units
    ]
    cumul = [cumulate(gate[t, w], rows, columns) for t, w in zip(tall, wide)]
    middle = [c[MID : MID + 1, :] for c in cumul]
    queries = [normalize(queries_all[t, w]) * DK ** (-0.5) for t, w in zip(tall, wide)]
    queried = [q * jnp.exp(c - m) for q, c, m in zip(queries, cumul, middle)]
    scores = [mm(q, f, NT, PASS_SCORES) for q, f in zip(queried, forward)]
    scores = [jnp.where(columns <= rows, x, 0.0) for x in scores]
    moved = [mm(x, u, NN, PASS_SU) for x, u in zip(scores, solved)]
    weights = [
        (q * jnp.exp(m) - x[:, :DK]).astype(BF16) for q, m, x in zip(queried, middle, moved)
    ]
    later = [
        dot(w, carry[first_head + i], NT) if c == 1 else None for (i, c), w in zip(units, weights)
    ]
    for (i, c), t, w, weight, x, extra in zip(units, tall, wide, weights, moved, later):
        direct = x[:, DK:]
        if c == 1:
            direct = direct + extra[:, DK:]
            weight = extra[:, :DK].astype(BF16)
        direct_out[t, w] = direct
        coefficient_out[t, w] = weight
    if kept:
        fetch.wait()


def scan_kernel(slots, where, *refs):
    count = len(slots)
    tables, outs, (states, table) = refs[:count], refs[count:-2], refs[-2:]
    for slot, ref in zip(slots, tables):
        table[slot] = ref[...]
    state = jnp.zeros((DK, DK), F32)
    for shard in range(count):
        slot = lax.bitwise_xor(where[0], shard)
        states[slot] = state.astype(BF16)
        if shard < count - 1:
            high = table[slot, 2 * DK : 2 * DK + 1, :].astype(F32)
            low = table[slot, 2 * DK + 8 : 2 * DK + 9, :].astype(F32)
            state = (
                state * (high + low)
                - dot(state.astype(BF16), table[slot, 0:DK, :], NN)
                + table[slot, DK : 2 * DK, :].astype(F32)
            )
    for pair, out in enumerate(outs):
        out[...] = states[2 * pair : 2 * pair + 2]


def fetch_kernel(source, out, arrived):
    copy = pltpu.make_async_copy(source.at[:, 0 : out.shape[1]], out, arrived)
    copy.start()
    copy.wait()


def gather_kernel(*refs):
    *pairs, out = refs
    for i, pair in enumerate(pairs):
        out[i] = pair[1]


def tail_kernel(query, key, value, out):
    out[0] = query[...]
    out[1] = key[...]
    out[2] = value[...]


def project_kernel(heads, owners, where, mine, direct_one, direct_two, weight_one, weight_two, early, matrix, *rest):
    arrived, rest = rest[: heads // 2 + 1], rest[heads // 2 + 1 :]
    *outs, head_out, ordered, states, late, landed = rest
    half_width = early.shape[1]
    copy = pltpu.make_async_copy(matrix.at[:, half_width:], late, landed)
    copy.start()
    for pair in range(heads // 2):
        states[2 * pair] = arrived[pair][0]
        states[2 * pair + 1] = arrived[-1][pair]
    parts = len(owners)
    share = head_out.shape[0] // parts

    @pl.when(pl.program_id(0) == 0)
    def _():
        for head in range(heads):
            at = slice(head * DK, (head + 1) * DK)
            half, inner = divmod(head, heads // 2)
            near = slice(inner * DK, (inner + 1) * DK)
            slot = lax.bitwise_xor(where[0], head)
            total = (direct_one, direct_two)[half][:, near] + dot(
                (weight_one, weight_two)[half][:, near], states[slot], NT
            )
            head_out[:, at] = total.astype(BF16)
        for distance in range(parts):
            owner = owners[distance](mine[0])
            ordered[distance * share : (distance + 1) * share, :] = head_out[
                pl.ds(pl.multiple_of(owner * share, share), share), :
            ]

    for side in range(2):
        if side == 1:
            copy.wait()
        total = dot(ordered[...], (early, late)[side][...], NN)
        at = slice(side * half_width, side * half_width + total.shape[1])
        for distance in range(parts):
            outs[distance][:, at] = total[distance * share : (distance + 1) * share, :].astype(
                outs[distance].dtype
            )


def spec(shape, index):
    return pl.BlockSpec(shape, index)


def call(kernel, grid, in_specs, out_specs, out_shape, scratch, cost, limit, scalars, *args):
    return pl.pallas_call(
        kernel,
        grid_spec=pltpu.PrefetchScalarGridSpec(
            num_scalar_prefetch=scalars,
            grid=grid,
            in_specs=in_specs,
            out_specs=out_specs,
            scratch_shapes=scratch,
        ),
        out_shape=out_shape,
        compiler_params=pltpu.CompilerParams(
            dimension_semantics=("arbitrary",) * len(grid), vmem_limit_bytes=limit << 20
        ),
        cost_estimate=pl.CostEstimate(flops=cost[0], bytes_accessed=cost[1], transcendentals=0),
    )(*args)


def shards(query, key_in, value, gates, beta, conv_query, conv_key, conv_value, out_weight):
    length, width = query.shape
    groups = beta.shape[1]
    taps = conv_query.shape[0]
    ranks = lax.axis_size("seq")
    me = lax.axis_index("seq").astype(jnp.int32)
    spread = groups == ranks
    order = me if spread else jnp.zeros((), jnp.int32)
    shape = jax.ShapeDtypeStruct
    kept = pltpu.VMEM
    here = pl.BlockSpec(memory_space=pltpu.VMEM)
    anywhere = pl.BlockSpec(memory_space=pl.ANY)
    query, key_in, value, gates, beta_rows, conv_query, conv_key, conv_value, out_weight = (
        pltpu.with_memory_space_constraint(data, pltpu.HBM)
        for data in (
            query, key_in, value, gates, beta.T, conv_query, conv_key, conv_value, out_weight
        )
    )
    tail_spec = spec((HALO, width), lambda p: (length // HALO - 1, 0))
    rims = call(
        tail_kernel, (1,), [tail_spec] * 3,
        spec((3, HALO, width), lambda p: (0, 0, 0)), shape((3, HALO, width), BF16),
        [], (0, 3 * HALO * width * 4), LIMIT, 0, query, key_in, value,
    )
    rims = lax.ppermute(rims, "seq", [(i, i + 1) for i in range(ranks - 1)])

    def chunk_specs(c):
        return [spec((CHUNK, width), lambda p, *_: (c, 0))] * 3 + [
            spec((groups, CHUNK), lambda p, *_: (0, c))
        ]

    tap_spec = spec((taps, width), lambda p, *_: (0, 0))
    rim_spec = spec((HALO, width), lambda p, *_: (CHUNK // HALO - 1, 0))
    solved_shape = kept((groups, CHUNK, 2 * DK), F32)
    forward_shape = kept((CHUNK, width), BF16 if PASS_SCORES == 1 else F32)
    conv_scratch = pltpu.VMEM((2, 8 + CHUNK, width), F32)
    cost = (groups * 100_000_000, 4 << 20)

    later_summary, later_decay, later_solved, later_forward = call(
        later_kernel,
        (1,),
        chunk_specs(1) + [rim_spec, rim_spec, tap_spec, tap_spec],
        [here] * 4,
        [kept((groups, 2 * DK, DK), F32), kept((groups, 8, DK), F32), solved_shape, forward_shape],
        [conv_scratch],
        cost,
        LIMIT,
        0,
        key_in, value, gates, beta_rows, key_in, value, conv_key, conv_value,
    )
    packed = 2 * DK + 16
    carry, first_solved, first_forward, *send = call(
        first_kernel,
        (1,),
        chunk_specs(0) + [here, tap_spec, tap_spec, here, here],
        [here] * (3 + groups),
        [kept((groups, 2 * DK, DK), BF16), solved_shape, forward_shape]
        + [kept((packed, DK), BF16)] * groups,
        [pltpu.VMEM((groups, packed, DK), BF16), conv_scratch],
        cost,
        LIMIT,
        1,
        order[None], key_in, value, gates, beta_rows, rims, conv_key, conv_value,
        later_summary, later_decay,
    )

    hops = sorted(range(1, ranks), key=lambda m: (-(m // 2).bit_count(), m))

    def exchange(blocks):
        sent = [lax.ppermute(blocks[m], "seq", [(i, i ^ m) for i in range(ranks)]) for m in hops]
        return [blocks[0]] + sent

    def outputs(half, later_solved, fetch):
        half_spec = spec((length, width // 2), lambda p: (0, half))
        extra_shape = [kept(out_weight.shape, BF16)] if fetch else []
        return call(
            functools.partial(output_kernel, half * groups // 2),
            (1,),
            [half_spec, half_spec, here, spec((taps, width // 2), lambda p: (0, half))]
            + [here] * 5
            + [pl.BlockSpec(memory_space=pl.ANY)],
            [here] * (3 if fetch else 2),
            [kept((length, width // 2), F32), kept((length, width // 2), BF16)] + extra_shape,
            ([pltpu.SemaphoreType.DMA] if fetch else [])
            + [pltpu.VMEM((8 + length, width // 2), F32)],
            (groups * 50_000_000, 2 << 20),
            LIMIT,
            0,
            query, gates, rims, conv_query,
            first_solved, later_solved, first_forward, later_forward, carry, out_weight,
        )

    direct_one, weight_one = outputs(0, later_solved, False)
    if spread:
        arrived = exchange(send)
        arrived, direct_one, weight_one = lax.optimization_barrier((arrived, direct_one, weight_one))
        states = call(
            functools.partial(scan_kernel, [0] + hops),
            (1,),
            [here] * ranks,
            [here] * (ranks // 2),
            [shape((2, DK, DK), BF16)] * (ranks // 2),
            [pltpu.VMEM((ranks, DK, DK), BF16), pltpu.VMEM((ranks, packed, DK), BF16)],
            (ranks * 4_000_000, 1 << 20),
            LIMIT,
            1,
            me[None], *arrived,
        )
        states, later_solved = lax.optimization_barrier((states, later_solved))
        direct_two, weight_two = outputs(1, later_solved, False)
        states = [states[0]] + [
            lax.ppermute(states[d], "seq", [(i, i ^ (2 * d)) for i in range(ranks)])
            for d in range(1, ranks // 2)
        ]
        states, direct_two, weight_two = lax.optimization_barrier((states, direct_two, weight_two))
        aside = call(
            gather_kernel, (1,), [here] * (ranks // 2), here,
            shape((ranks // 2, DK, DK), BF16), [], (0, 1 << 18), LIMIT, 0, *states,
        )
        aside, source = lax.optimization_barrier((aside, out_weight))
        states = states + [lax.ppermute(aside, "seq", [(i, i ^ 1) for i in range(ranks)])]
    else:
        direct_two, weight_two = outputs(1, later_solved, False)
        every = lax.all_gather(jnp.stack(send), "seq")
        product, offset = every[:, :, :DK].astype(F32), every[:, :, DK : 2 * DK].astype(F32)
        decay = every[:, :, 2 * DK : 2 * DK + 1].astype(F32) + every[:, :, 2 * DK + 8 : 2 * DK + 9].astype(F32)
        state = jnp.zeros((groups, DK, DK), F32)
        states = state
        for shard in range(ranks):
            states = jnp.where(me == shard, state, states)
            moved = jnp.einsum("hij,hjk->hik", state, product[shard], precision=lax.Precision.HIGHEST)
            state = state * decay[shard] - moved + offset[shard]
        states = states.astype(BF16)
        source = out_weight
        states = [states[i : i + 2] for i in range(0, groups, 2)] + [states[1::2]]

    parts = lax.axis_size("head")
    mine = lax.axis_index("head").astype(jnp.int32)
    share = length // parts
    model = out_weight.shape[1]
    if parts == 4:
        owners = (
            lambda z: z,
            lambda z: jnp.where(lax.rem(z, 2) == 0, 3, 0),
            lambda z: jnp.where(z < 2, 2, 1),
            lambda z: lax.rem(2 * z + 1, 5),
        )
    else:
        owners = [lambda z, d=d: lax.rem(z + d, parts) for d in range(parts)]
    half = 8 * (model // 9)
    early = call(
        fetch_kernel, (1,), [anywhere], here, kept((width, half), BF16),
        [pltpu.SemaphoreType.DMA], (0, width * model * 2), LIMIT, 0, source,
    )
    own, *leaving = call(
        functools.partial(project_kernel, groups, owners),
        (1,),
        [here] * 5 + [anywhere] + [here] * (groups // 2 + 1),
        [here] * parts,
        [kept((share, model), F32)] + [kept((share, model), BF16)] * (parts - 1),
        [pltpu.VMEM((length, width), BF16)] * 2
        + [
            pltpu.VMEM((groups, DK, DK), BF16),
            pltpu.VMEM((width, model - half), BF16),
            pltpu.SemaphoreType.DMA,
        ],
        (2 * length * width * model, width * model * 2),
        LIMIT,
        2,
        order[None], mine[None], direct_one, direct_two, weight_one, weight_two, early, source, *states,
    )
    if parts == 4:
        near, inward, last = leaving
        middle = (mine == 1) | (mine == 2)
        near = lax.ppermute(near, "head", [(0, 1), (1, 0), (2, 3), (3, 2)]).astype(F32)
        crossed = lax.ppermute(inward, "head", [(1, 2), (2, 1)])
        skipped = lax.ppermute(inward, "head", [(0, 2), (3, 1)])
        joined = (last.astype(F32) + jnp.where(middle, near, 0.0)).astype(BF16)
        joined = lax.ppermute(joined, "head", [(0, 1), (3, 2), (1, 3), (2, 0)])
        arrived = [jnp.where(middle, 0.0, near), crossed, skipped, joined]
    else:
        arrived = [
            lax.ppermute(part, "head", [(i, (i + d) % parts) for i in range(parts)])
            for d, part in enumerate(leaving, 1)
        ]
    total = own
    for part in arrived:
        total = total + part.astype(F32)
    return total.astype(BF16)


def solution(mesh):
    in_specs = (
        P("seq", "head"),
        P("seq", "head"),
        P("seq", "head"),
        P("seq", "head"),
        P("seq", "head"),
        P(None, "head"),
        P(None, "head"),
        P(None, "head"),
        P("head", None),
    )
    out_specs = P(("seq", "head"), None)
    return jax.shard_map(shards, mesh=mesh, in_specs=in_specs, out_specs=out_specs, check_vma=False)
```
